32 devices in a mesh: groups: 2 (over x), tm: 8 (over z, y), rows: 2 (over core).
Axes of the slice: x: 2, y: 2, z: 4, core: 2. Of those that a mesh axis runs over, the one named last changes fastest.
Arguments:
- frames_in: bfloat16 [4, 8, 16, 256, 128], P('groups', 'tm', 'rows'), parts along dimension 0, may hold values from -12 to 12
- gain_one: float32 [128], replicated, may hold values from 0.25 to 1.75
- norm_bias_one: float32 [128], replicated, may hold values from -3 to 3
- kernel_one: bfloat16 [3, 3, 3, 128, 128], replicated, may hold values from -0.109375 to 0.109375
- bias_one: float32 [128], replicated, may hold values from -2 to 2
- gain_two: float32 [128], replicated, may hold values from 0.25 to 1.75
- norm_bias_two: float32 [128], replicated, may hold values from -3 to 3
- kernel_two: bfloat16 [3, 3, 3, 128, 128], replicated, may hold values from -0.109375 to 0.109375
- bias_two: float32 [128], replicated, may hold values from -2 to 2
- kernel_down: bfloat16 [3, 3, 128, 128], replicated, may hold values from -0.1875 to 0.1875
- bias_down: float32 [128], replicated, may hold values from -2 to 2
Outputs:
- features_down: bfloat16 [4, 8, 8, 128, 128], P('groups', 'tm', 'rows'), parts along dimension 0
The draws below stay inside these ranges and needn't reach their ends.
There are 2 independent parts, one for each index of `groups`. The reference program is written for one: setup_inputs(seed, part) draws one part's arguments, and reference() takes and returns one part's arrays. A program takes and returns all parts, laid end to end along the dimension named above; an argument that names none is the same for every part. Nothing has to cross between parts.
All inputs are finite; a program needn't handle non-finite values.
Results may differ from the reference program's by a relative error of at most 0.0095.
Values may be sent and summed in bfloat16 or wider, within the bound.
No kernel may reach another device: no remote copies, remote signals or barrier semaphores. Data moves between devices by JAX's collectives and lax.ppermute only.
A program may use at most 128 MiB of HBM per device.

```python
import jax
import jax.numpy as jnp
from jax import lax

C = 128
G = 32
CLIPS = 2
W = 256
FRAMES = 8
H = 16


def draw_frames_in(key, part):
    key_base = jax.random.fold_in(key, 11)
    key_frame = jax.random.fold_in(key, 12)
    key_offset = jax.random.fold_in(key, 13)
    shape = (CLIPS, FRAMES, H, W, C)
    positions = jnp.arange(H, dtype=jnp.float32) / (H - 1)
    frame_scale = jax.random.uniform(key_frame, (CLIPS, FRAMES, 1, 1, 1), minval=0.5, maxval=1.5)
    offset = 0.3 * jax.random.normal(key_offset, (CLIPS, FRAMES, 1, 1, C))
    base = jax.random.normal(key_base, shape)
    row_scale = 0.6 * jnp.exp(jnp.log(3.0) * positions)
    values = base * frame_scale * row_scale[None, None, :, None, None] + offset
    return jnp.clip(values, -12.0, 12.0).astype(jnp.bfloat16)


def bell_draw(stream_key, dims, scale, most, kind=jnp.bfloat16):
    drawn = jax.random.normal(stream_key, dims, jnp.float32) * scale
    return jnp.minimum(jnp.maximum(drawn, -most), most).astype(kind)


def setup_inputs(seed: int = 0, part: int = 0) -> dict:
    seeds = jax.random.split(jax.random.key(seed), 12)
    own_keys = jax.random.split(jax.random.fold_in(seeds[11], part), 12)
    frames_in = draw_frames_in(jax.random.fold_in(jax.random.fold_in(seeds[11], part), 71), part)
    gain_one = jnp.clip(1.0 + 0.15 * jax.random.normal(seeds[1], (C,), jnp.float32), 0.25, 1.75)
    norm_bias_one = bell_draw(seeds[2], (C,), 0.5, 3.0, jnp.float32)
    kernel_one = bell_draw(seeds[3], (3, 3, 3, C, C), (27 * C) ** -0.5, 0.109375)
    bias_one = bell_draw(seeds[4], (C,), 0.3, 2.0, jnp.float32)
    gain_two = jnp.clip(1.0 + 0.15 * jax.random.normal(seeds[5], (C,), jnp.float32), 0.25, 1.75)
    norm_bias_two = bell_draw(seeds[6], (C,), 0.5, 3.0, jnp.float32)
    kernel_two = bell_draw(seeds[7], (3, 3, 3, C, C), (27 * C) ** -0.5, 0.109375)
    bias_two = bell_draw(seeds[8], (C,), 0.3, 2.0, jnp.float32)
    kernel_down = bell_draw(seeds[9], (3, 3, C, C), (9 * C) ** -0.5, 0.1875)
    bias_down = bell_draw(seeds[10], (C,), 0.3, 2.0, jnp.float32)
    return {"frames_in": frames_in, "gain_one": gain_one, "norm_bias_one": norm_bias_one, "kernel_one": kernel_one, "bias_one": bias_one, "gain_two": gain_two, "norm_bias_two": norm_bias_two, "kernel_two": kernel_two, "bias_two": bias_two, "kernel_down": kernel_down, "bias_down": bias_down}


EPSILON = 1e-06

def normalize(values, gain, bias):
    batch, frames, height, width, channels = values.shape
    grouped = values.reshape(batch, frames, height, width, G, channels // G)
    average = lax.optimization_barrier(jnp.mean(grouped, axis=(2, 3, 5), keepdims=True))
    mean_square = lax.optimization_barrier(jnp.mean(grouped * grouped, axis=(2, 3, 5), keepdims=True))
    inverse = lax.rsqrt(mean_square - average * average + EPSILON)
    scaled = ((grouped - average) * inverse).reshape(values.shape) * gain + bias
    return jax.nn.silu(scaled).astype(jnp.bfloat16)

def causal_conv(normed, kernel, bias):
    batch, frames, height, width, channels = normed.shape
    values = normed.astype(jnp.float32)
    padded = jnp.concatenate([values[:, :1], values[:, :1], values], axis=1)
    stacked = jnp.concatenate([padded[:, 0:frames], padded[:, 1:frames + 1], padded[:, 2:frames + 2]], axis=-1)
    stacked = stacked.reshape(batch * frames, height, width, 3 * channels)
    weights = kernel.astype(jnp.float32).reshape(3, 3, 3 * channels, channels)
    result = lax.conv_general_dilated(stacked, weights, (1, 1), ((1, 1), (1, 1)), dimension_numbers=('NHWC', 'HWIO', 'NHWC'), precision=lax.Precision.HIGHEST, preferred_element_type=jnp.float32)
    return result.reshape(batch, frames, height, width, channels) + bias

def reference(frames_in, gain_one, norm_bias_one, kernel_one, bias_one, gain_two, norm_bias_two, kernel_two, bias_two, kernel_down, bias_down):
    batch, frames, height, width, channels = frames_in.shape
    inputs = frames_in.astype(jnp.float32)
    hidden_one = causal_conv(normalize(inputs, gain_one, norm_bias_one), kernel_one, bias_one).astype(jnp.bfloat16)
    normed_two = normalize(hidden_one.astype(jnp.float32), gain_two, norm_bias_two)
    residual = (inputs + causal_conv(normed_two, kernel_two, bias_two)).astype(jnp.bfloat16)
    flat = residual.astype(jnp.float32).reshape(batch * frames, height, width, channels)
    padded = jnp.pad(flat, ((0, 0), (0, 1), (0, 1), (0, 0)))
    result = lax.conv_general_dilated(padded, kernel_down.astype(jnp.float32), (2, 2), 'VALID', dimension_numbers=('NHWC', 'HWIO', 'NHWC'), precision=lax.Precision.HIGHEST, preferred_element_type=jnp.float32)
    result = result + bias_down
    return result.reshape(batch, frames, height // 2, width // 2, channels).astype(jnp.bfloat16)
```

```python
import functools

import jax
import jax.numpy as jnp
from jax import lax
from jax.experimental import pallas as pl
from jax.experimental.pallas import tpu as pltpu
from jax.sharding import PartitionSpec as P

G = 32
EPSILON = 1e-06
F32 = jnp.float32
BF16 = jnp.bfloat16


def norm_params(totals, gain, bias, cells):
    channels = totals.shape[1]
    size = channels // G
    left = lax.broadcasted_iota(jnp.int32, (channels, channels), 0) // size
    right = lax.broadcasted_iota(jnp.int32, (channels, channels), 1) // size
    same = (left == right).astype(F32)
    grouped = jnp.dot(totals, same, precision=lax.Precision.HIGHEST, preferred_element_type=F32)
    grouped = grouped / (cells * size)
    mean = grouped[0:1]
    inverse = lax.rsqrt(grouped[1:2] - mean * mean + EPSILON)
    return mean, inverse * gain, bias


def fill_row(stack, r, values, params, keep=None):
    mean, scale, bias = params
    width, channels = values.shape
    half = 0.5 * ((values.astype(F32) - mean) * scale + bias)
    normed = half + half * jnp.tanh(half)
    if keep is not None:
        normed = jnp.where(keep, normed, 0.0)
    column = lax.broadcasted_iota(jnp.int32, (width, channels), 0)
    before = jnp.where(column == 0, 0.0, pltpu.roll(normed, 1, 0))
    after = jnp.where(column == width - 1, 0.0, pltpu.roll(normed, width - 1, 0))
    stack[r, :, 0:channels] = before.astype(BF16)
    stack[r, :, channels : 2 * channels] = normed.astype(BF16)
    stack[r, :, 2 * channels :] = after.astype(BF16)


def fill_rows(stack, rows, read, halo, params, band):
    height, edges, last = rows
    for r in range(height + 1 + last):
        if r == 0:
            fill_row(stack, r, halo(edges - 1), params, band == 1)
        elif r <= height:
            fill_row(stack, r, read(r - 1), params)
        else:
            fill_row(stack, r, halo(r - 1 - height), params, band == 0)


def taps(stack, weights, start, count):
    rows = [
        jnp.concatenate([stack[r], stack[r + 1], stack[r + 2]], axis=1)
        for r in range(start, start + count)
    ]
    return jnp.dot(jnp.concatenate(rows, axis=0), weights, preferred_element_type=F32)


def steps(total):
    size = 3 if total % 3 == 0 else 2
    return [(r, min(size, total - r)) for r in range(0, total, size)]


def sums_kernel(x_ref, out_ref):
    clips, height, width, channels = x_ref.shape
    for c in range(clips):
        total = jnp.zeros((8, channels), F32)
        square = jnp.zeros((8, channels), F32)
        for r in range(height):
            v = x_ref[c, r].astype(F32).reshape(width // 8, 8, channels)
            total += jnp.sum(v, axis=0)
            square += jnp.sum(v * v, axis=0)
        out_ref[c, 0:1] = jnp.sum(total, axis=0, keepdims=True)
        out_ref[c, 1:2] = jnp.sum(square, axis=0, keepdims=True)
        out_ref[c, 2:8] = jnp.zeros((6, channels), F32)


def local_kernel(cells, flags, a_ref, b_ref, ha_ref, hb_ref, ta_ref, tb_ref, g_ref, c_ref, wa_ref, wb_ref, acc_ref, xa, xb):
    band = flags[2]
    out_rows, width, _ = acc_ref.shape
    height = a_ref.shape[0]
    edges = ha_ref.shape[0]
    rows = (height, edges, out_rows + 1 - height)
    pa = norm_params(ta_ref[...], g_ref[...], c_ref[...], cells)
    pb = norm_params(tb_ref[...], g_ref[...], c_ref[...], cells)
    fill_rows(xa, rows, lambda r: a_ref[r], lambda r: ha_ref[r], pa, band)
    fill_rows(xb, rows, lambda r: b_ref[r], lambda r: hb_ref[r], pb, band)
    for start, count in steps(out_rows):
        part = taps(xa, wa_ref[...], start, count) + taps(xb, wb_ref[...], start, count)
        acc_ref[start : start + count] = part.reshape(count, width, -1)


def fill_earlier(stack, cells, flags, refs, out_rows):
    p_ref, hp_ref, tp_ref, a_ref, ha_ref, ta_ref, g_ref, c_ref = refs
    first = flags[1] == 1
    height = p_ref.shape[0]
    rows = (height, hp_ref.shape[0], out_rows + 1 - height)
    params = norm_params(jnp.where(first, ta_ref[...], tp_ref[...]), g_ref[...], c_ref[...], cells)
    fill_rows(
        stack,
        rows,
        lambda r: jnp.where(first, a_ref[r], p_ref[r]),
        lambda r: jnp.where(first, ha_ref[r], hp_ref[r]),
        params,
        flags[2],
    )


def middle_kernel(cells, flags, *refs):
    *frame, w_ref, in_ref, acc_ref, stack = refs
    out_rows, width, _ = acc_ref.shape
    fill_earlier(stack, cells, flags, frame, out_rows)
    for start, count in steps(out_rows):
        part = taps(stack, w_ref[...], start, count).reshape(count, width, -1)
        acc_ref[start : start + count] = in_ref[start : start + count] + part


def hidden_kernel(cells, flags, *refs):
    *frame, w_ref, in_ref, bias_ref, a_ref, b_ref, sum_ref, stack = refs
    out_rows, width, both = in_ref.shape
    channels = both // 2
    fill_earlier(stack, cells, flags, frame, out_rows)
    total = jnp.zeros((8, both), F32)
    square = jnp.zeros((8, both), F32)
    for start, count in steps(out_rows):
        part = taps(stack, w_ref[...], start, count).reshape(count, width, both)
        hidden = (in_ref[start : start + count] + part + bias_ref[...]).astype(BF16)
        a_ref[start : start + count] = hidden[:, :, :channels]
        b_ref[start : start + count] = hidden[:, :, channels:]
        wide = hidden.astype(F32).reshape(count * width // 8, 8, both)
        total += jnp.sum(wide, axis=0)
        square += jnp.sum(wide * wide, axis=0)
    total = jnp.sum(total, axis=0, keepdims=True)
    square = jnp.sum(square, axis=0, keepdims=True)
    for k in range(2):
        sum_ref[k, 0:1] = total[:, k * channels : (k + 1) * channels]
        sum_ref[k, 1:2] = square[:, k * channels : (k + 1) * channels]
        sum_ref[k, 2:8] = jnp.zeros((6, channels), F32)


def down_kernel(cells, flags, *refs):
    (*frame, w_ref, in_ref, bias_ref, xa_ref, xb_ref, ea_ref, eb_ref, wd_ref, bd_ref, out_ref, stack, res) = refs
    out_rows, width, both = in_ref.shape
    channels = both // 2
    band = flags[2]
    fill_earlier(stack, cells, flags, frame, out_rows)
    height = out_rows - 1
    res[:, :, width:, :] = jnp.zeros((2, out_rows, res.shape[2] - width, channels), F32)
    for start, count in steps(out_rows):
        part = taps(stack, w_ref[...], start, count).reshape(count, width, both)
        branch = in_ref[start : start + count] + part + bias_ref[...]
        for k in range(count):
            r = start + k
            for f, (x_ref, e_ref) in enumerate(((xa_ref, ea_ref), (xb_ref, eb_ref))):
                raw = x_ref[r] if r < height else e_ref[0]
                value = raw.astype(F32) + branch[k, :, f * channels : (f + 1) * channels]
                value = value.astype(BF16).astype(F32)
                if r >= height:
                    value = jnp.where(band == 0, value, 0.0)
                res[f, r, 0:width, :] = value
    half = width // 2
    for f in range(2):
        rows = []
        for i in range(height // 2):
            cols = [
                res[f, 2 * i + a, pl.ds(b, half, stride=2), :].astype(BF16)
                for a in range(3)
                for b in range(3)
            ]
            rows.append(jnp.concatenate(cols, axis=1))
        out = jnp.dot(jnp.concatenate(rows, axis=0), wd_ref[...], preferred_element_type=F32)
        out_ref[f] = (out + bd_ref[...]).astype(BF16).reshape(height // 2, half, channels)


def call(kernel, out_shape, scratch, flags, *args, aliases=None, flops=0):
    vmem = pl.BlockSpec(memory_space=pltpu.VMEM)
    several = isinstance(out_shape, (list, tuple))
    moved = sum(a.size * a.dtype.itemsize for a in args)
    return pl.pallas_call(
        kernel,
        out_shape=out_shape,
        in_specs=[pl.BlockSpec(memory_space=pltpu.SMEM)] + [vmem] * len(args),
        out_specs=[vmem] * len(out_shape) if several else vmem,
        scratch_shapes=scratch,
        input_output_aliases=aliases or {},
        cost_estimate=pl.CostEstimate(flops=flops, bytes_accessed=moved, transcendentals=0),
        compiler_params=pltpu.CompilerParams(vmem_limit_bytes=32 << 20),
    )(flags, *args)


def slot_weights(kernel):
    channels = kernel.shape[-1]
    by_frame = jnp.transpose(kernel, (2, 0, 1, 3, 4)).reshape(3, -1, channels)
    padded = jnp.pad(by_frame, ((1, 1), (0, 0), (0, 0)))
    return jnp.concatenate([padded[1:], padded[:-1]], axis=-1)


def local(
    frames_in,
    gain_one,
    norm_bias_one,
    kernel_one,
    bias_one,
    gain_two,
    norm_bias_two,
    kernel_two,
    bias_two,
    kernel_down,
    bias_down,
):
    x = frames_in[:, 0]
    clips, height, width, channels = x.shape
    count = lax.axis_size("tm")
    bands = lax.axis_size("rows")
    assert clips == 2 and bands == 2 and count % 2 == 0
    cells = height * bands * width
    position = lax.axis_index("tm")
    band = lax.axis_index("rows")
    side = position % 2
    flags = jnp.stack([side, (position < 2).astype(jnp.int32), band]).astype(jnp.int32)
    swap = [(i, i ^ 1) for i in range(count)]
    onward = [(i, i + 2) for i in range(count - 2)]
    across = [(0, 1), (1, 0)]

    def swapped(v):
        return lax.ppermute(v, "tm", swap)

    def later(v):
        return lax.ppermute(v, "tm", onward)

    def beside(v):
        return lax.ppermute(v, "rows", across)

    def edge(v, edges):
        return jnp.where(band == 0, v[height - edges :], v[:edges])

    def pick(pair, index):
        return lax.dynamic_index_in_dim(pair, index, 0, keepdims=False)

    row = lambda v: v.reshape(1, -1)
    stack = lambda rows: pltpu.VMEM((rows, width, 3 * channels), BF16)
    flops = lambda rows, slots: 2 * rows * width * 9 * channels * 2 * channels * slots

    own = pick(x, side)
    other = pick(x, 1 - side)
    mate = swapped(other)
    own_before = later(own)
    mate_before = later(mate)

    partial = call_sums(x)
    totals = partial + beside(partial)
    own_total = pick(totals, side)
    mate_total = swapped(pick(totals, 1 - side))
    both_before = later(jnp.stack([own_total, mate_total]))

    own_edge = beside(edge(own, 1))
    mate_edge = beside(edge(mate, 1))
    own_before_edge = beside(edge(own_before, 1))
    mate_before_edge = beside(edge(mate_before, 1))

    weights = slot_weights(kernel_one)
    even = side == 0
    first_frame = jnp.where(even, own, mate)
    second_frame = jnp.where(even, mate, own)
    first_edge = jnp.where(even, own_edge, mate_edge)
    second_edge = jnp.where(even, mate_edge, own_edge)
    first_total = jnp.where(even, own_total, mate_total)
    second_total = jnp.where(even, mate_total, own_total)
    norm_one = (row(gain_one), row(norm_bias_one))

    acc_shape = jax.ShapeDtypeStruct((height, width, 2 * channels), F32)
    acc = call(
        functools.partial(local_kernel, cells),
        acc_shape,
        [stack(height + 2), stack(height + 2)],
        flags,
        first_frame,
        second_frame,
        first_edge,
        second_edge,
        first_total,
        second_total,
        *norm_one,
        weights[2],
        weights[3],
        flops=flops(height, 2),
    )
    fallback = (first_frame, first_edge, first_total)
    acc = call(
        functools.partial(middle_kernel, cells),
        acc_shape,
        [stack(height + 2)],
        flags,
        own_before,
        own_before_edge,
        both_before[0],
        *fallback,
        *norm_one,
        pick(weights, side),
        acc,
        flops=flops(height, 1),
    )
    frame_shape = jax.ShapeDtypeStruct((height, width, channels), BF16)
    hidden_a, hidden_b, partial = call(
        functools.partial(hidden_kernel, cells),
        [frame_shape, frame_shape, jax.ShapeDtypeStruct((2, 8, channels), F32)],
        [stack(height + 2)],
        flags,
        mate_before,
        mate_before_edge,
        both_before[1],
        *fallback,
        *norm_one,
        pick(weights, 1 - side),
        acc,
        row(jnp.tile(bias_one, 2)),
        flops=flops(height, 1),
    )

    before_b = later(hidden_b)
    before_a = later(hidden_a)
    totals = partial + beside(partial)
    totals_before = later(totals)
    edge_ab = beside(jnp.stack([edge(hidden_a, 2), edge(hidden_b, 2)]))
    before_b_edge = beside(edge(before_b, 2))
    before_a_edge = beside(edge(before_a, 2))

    weights = slot_weights(kernel_two)
    norm_two = (row(gain_two), row(norm_bias_two))
    acc_shape = jax.ShapeDtypeStruct((height + 1, width, 2 * channels), F32)
    acc = call(
        functools.partial(local_kernel, cells),
        acc_shape,
        [stack(height + 3), stack(height + 3)],
        flags,
        hidden_a,
        hidden_b,
        edge_ab[0],
        edge_ab[1],
        totals[0],
        totals[1],
        *norm_two,
        weights[2],
        weights[3],
        flops=flops(height + 1, 2),
    )
    fallback = (hidden_a, edge_ab[0], totals[0])
    acc = call(
        functools.partial(middle_kernel, cells),
        acc_shape,
        [stack(height + 3)],
        flags,
        before_b,
        before_b_edge,
        totals_before[1],
        *fallback,
        *norm_two,
        weights[1],
        acc,
        flops=flops(height + 1, 1),
    )
    out = call(
        functools.partial(down_kernel, cells),
        jax.ShapeDtypeStruct((2, height // 2, width // 2, channels), BF16),
        [stack(height + 3), pltpu.VMEM((2, height + 1, width + 8, channels), F32)],
        flags,
        before_a,
        before_a_edge,
        totals_before[0],
        *fallback,
        *norm_two,
        weights[0],
        acc,
        row(jnp.tile(bias_two, 2)),
        first_frame,
        second_frame,
        first_edge,
        second_edge,
        kernel_down.reshape(-1, channels),
        row(bias_down),
        flops=flops(height + 1, 1),
    )
    kept = pick(out, side)
    received = swapped(pick(out, 1 - side))
    result = jnp.where(even, jnp.stack([kept, received]), jnp.stack([received, kept]))
    return result[:, None]


def call_sums(x):
    clips, _, _, channels = x.shape
    vmem = pl.BlockSpec(memory_space=pltpu.VMEM)
    return pl.pallas_call(
        sums_kernel,
        out_shape=jax.ShapeDtypeStruct((clips, 8, channels), F32),
        in_specs=[vmem],
        out_specs=vmem,
        cost_estimate=pl.CostEstimate(flops=4 * x.size, bytes_accessed=2 * x.size, transcendentals=0),
    )(x)


def solution(mesh):
    placed = (P("groups", "tm", "rows", None, None),) + (P(),) * 10
    return jax.shard_map(
        local,
        mesh=mesh,
        in_specs=placed,
        out_specs=P("groups", "tm", "rows", None, None),
        check_vma=False,
    )
```

```python
import functools

import jax
import jax.numpy as jnp
from jax import lax
from jax.experimental import pallas as pl
from jax.experimental.pallas import tpu as pltpu
from jax.sharding import PartitionSpec as P


G = 32
EPSILON = 1e-06
F32 = jnp.float32
BF16 = jnp.bfloat16


def norm_params(totals, gain, bias, cells):
    channels = totals.shape[1]
    size = channels // G
    left = lax.broadcasted_iota(jnp.int32, (channels, channels), 0) // size
    right = lax.broadcasted_iota(jnp.int32, (channels, channels), 1) // size
    same = (left == right).astype(F32)
    grouped = jnp.dot(totals, same, precision=lax.Precision.HIGHEST, preferred_element_type=F32)
    grouped = grouped / (cells * size)
    mean = grouped[0:1]
    inverse = lax.rsqrt(grouped[1:2] - mean * mean + EPSILON)
    return mean, inverse * gain, bias


def fill_row(stack, r, values, params):
    mean, scale, bias = params
    width, channels = values.shape
    half = 0.5 * ((values.astype(F32) - mean) * scale + bias)
    normed = half + half * jnp.tanh(half)
    column = lax.broadcasted_iota(jnp.int32, (width, channels), 0)
    before = jnp.where(column == 0, 0.0, pltpu.roll(normed, 1, 0))
    after = jnp.where(column == width - 1, 0.0, pltpu.roll(normed, width - 1, 0))
    stack[r, :, 0:channels] = before.astype(BF16)
    stack[r, :, channels : 2 * channels] = normed.astype(BF16)
    stack[r, :, 2 * channels :] = after.astype(BF16)


def fill_frame(stack, values, params):
    for r, value in enumerate(values):
        fill_row(stack, r, value(), params)


def close_stack(stack):
    last = stack.shape[0] - 1
    stack[last] = jnp.zeros(stack.shape[1:], BF16)


def taps(stack, weights, start, count):
    rows = [
        jnp.concatenate([stack[r], stack[r + 1], stack[r + 2]], axis=1)
        for r in range(start, start + count)
    ]
    return jnp.dot(jnp.concatenate(rows, axis=0), weights, preferred_element_type=F32)


def steps(first, last):
    total = last - first
    size = 3 if total % 3 == 0 else 2
    return [(r, min(size, last - r)) for r in range(first, last, size)]


def reader(ref, r):
    return lambda: ref[r]


def choose(flags, r, part, k, own, mate):
    def read():
        return jnp.where(flags[1] == 1, jnp.where(flags[0] == 0, own[r], mate[r]), part[k])

    return read


def place_kernel(flags, x_ref, own_ref, other_ref):
    height = x_ref.shape[1]
    side, band = flags[0], flags[2]
    for r in range(height):
        row = jnp.where(band == 0, height - 1 - r, r)
        own_ref[r] = x_ref[side, row]
        other_ref[r] = x_ref[1 - side, row]


def sums_kernel(x_ref, out_ref):
    clips, height, width, channels = x_ref.shape
    for c in range(clips):
        total = jnp.zeros((8, channels), F32)
        square = jnp.zeros((8, channels), F32)
        for r in range(height):
            v = x_ref[c, r].astype(F32).reshape(width // 8, 8, channels)
            total += jnp.sum(v, axis=0)
            square += jnp.sum(v * v, axis=0)
        out_ref[c, 0:1] = jnp.sum(total, axis=0, keepdims=True)
        out_ref[c, 1:2] = jnp.sum(square, axis=0, keepdims=True)
        out_ref[c, 2:8] = jnp.zeros((6, channels), F32)


def own_kernel(cells, flags, x_ref, e_ref, t_ref, g_ref, c_ref, w_ref, acc_ref, stack):
    height, width, _ = x_ref.shape
    params = norm_params(t_ref[...], g_ref[...], c_ref[...], cells)
    fill_frame(stack, [reader(e_ref, 0)] + [reader(x_ref, r) for r in range(height)], params)
    close_stack(stack)
    for start, count in steps(0, height):
        part = taps(stack, w_ref[...], start, count)
        acc_ref[start : start + count] = part.reshape(count, width, -1)


def mates_kernel(cells, flags, m_ref, em_ref, tm_ref, p_ref, ep_ref, tp_ref, o_ref, eo_ref, to_ref, g_ref, c_ref, wm_ref, wp_ref, in_ref, acc_ref, xm, xp):
    height, width, _ = m_ref.shape
    first, even = flags[1] == 1, flags[0] == 0
    params = norm_params(tm_ref[...], g_ref[...], c_ref[...], cells)
    fill_frame(xm, [reader(em_ref, 0)] + [reader(m_ref, r) for r in range(height)], params)
    close_stack(xm)
    totals = jnp.where(first, jnp.where(even, to_ref[...], tm_ref[...]), tp_ref[...])
    params = norm_params(totals, g_ref[...], c_ref[...], cells)
    values = [choose(flags, 0, ep_ref, 0, eo_ref, em_ref)]
    values += [choose(flags, r, p_ref, r, o_ref, m_ref) for r in range(height)]
    fill_frame(xp, values, params)
    close_stack(xp)
    for start, count in steps(0, height):
        part = taps(xm, wm_ref[...], start, count) + taps(xp, wp_ref[...], start, count)
        acc_ref[start : start + count] = in_ref[start : start + count] + part.reshape(count, width, -1)


def hidden_rows(stack, w_ref, in_ref, bias_ref, first, a_ref, b_ref, sum_ref):
    rows, width, channels = a_ref.shape
    both = 2 * channels
    total = jnp.zeros((8, both), F32)
    square = jnp.zeros((8, both), F32)
    for start, count in steps(0, rows):
        part = taps(stack, w_ref[...], start, count).reshape(count, width, both)
        begin = first + start
        hidden = (in_ref[begin : begin + count] + part + bias_ref[...]).astype(BF16)
        a_ref[start : start + count] = hidden[:, :, :channels]
        b_ref[start : start + count] = hidden[:, :, channels:]
        wide = hidden.astype(F32).reshape(count * width // 8, 8, both)
        total += jnp.sum(wide, axis=0)
        square += jnp.sum(wide * wide, axis=0)
    total = jnp.sum(total, axis=0, keepdims=True)
    square = jnp.sum(square, axis=0, keepdims=True)
    for k in range(2):
        sum_ref[k, 0:1] = total[:, k * channels : (k + 1) * channels]
        sum_ref[k, 1:2] = square[:, k * channels : (k + 1) * channels]
        sum_ref[k, 2:8] = jnp.zeros((6, channels), F32)


def near_kernel(cells, flags, p_ref, ep_ref, tp_ref, o_ref, eo_ref, to_ref, m_ref, em_ref, tm_ref, g_ref, c_ref, w_ref, in_ref, bias_ref, a_ref, b_ref, edge_ref, sum_ref, stack):
    totals = jnp.where(flags[1] == 1, jnp.where(flags[0] == 0, to_ref[...], tm_ref[...]), tp_ref[...])
    params = norm_params(totals, g_ref[...], c_ref[...], cells)
    values = [choose(flags, 0, ep_ref, 0, eo_ref, em_ref)]
    values += [choose(flags, r, p_ref, r, o_ref, m_ref) for r in range(p_ref.shape[0])]
    fill_frame(stack, values, params)
    hidden_rows(stack, w_ref, in_ref, bias_ref, 0, a_ref, b_ref, sum_ref)
    edge_ref[0] = a_ref[0:2]
    edge_ref[1] = b_ref[0:2]


def far_kernel(cells, flags, p_ref, q_ref, tp_ref, o_ref, to_ref, m_ref, tm_ref, g_ref, c_ref, w_ref, in_ref, bias_ref, a_ref, b_ref, sum_ref, stack):
    totals = jnp.where(flags[1] == 1, jnp.where(flags[0] == 0, to_ref[...], tm_ref[...]), tp_ref[...])
    params = norm_params(totals, g_ref[...], c_ref[...], cells)
    height, near = o_ref.shape[0], p_ref.shape[0]
    rows = a_ref.shape[0]
    values = []
    for r in range(height - rows - 1, height):
        part, k = (p_ref, r) if r < near else (q_ref, r - near)
        values.append(choose(flags, r, part, k, o_ref, m_ref))
    fill_frame(stack, values, params)
    close_stack(stack)
    hidden_rows(stack, w_ref, in_ref, bias_ref, height - rows, a_ref, b_ref, sum_ref)


def halves(edge, k, near, far):
    rows = [lambda: edge[k, 1], lambda: edge[k, 0]]
    rows += [reader(near, r) for r in range(near.shape[0])]
    return rows + [reader(far, r) for r in range(far.shape[0])]


def local_kernel(cells, flags, a1, a2, b1, b2, e_ref, t_ref, g_ref, c_ref, wa_ref, wb_ref, acc_ref, xa, xb):
    out_rows, width, _ = acc_ref.shape
    for k, (stack, near, far) in enumerate(((xa, a1, a2), (xb, b1, b2))):
        params = norm_params(t_ref[k], g_ref[...], c_ref[...], cells)
        fill_frame(stack, halves(e_ref, k, near, far), params)
        close_stack(stack)
    for start, count in steps(0, out_rows):
        part = taps(xa, wa_ref[...], start, count) + taps(xb, wb_ref[...], start, count)
        acc_ref[start : start + count] = part.reshape(count, width, -1)


def either(flags, first, other):
    return lambda: jnp.where(flags[1] == 1, first(), other())


def residual_row(raw, branch):
    return (raw.astype(F32) + branch).astype(BF16)


def put_row(res, r, value):
    res[r, 0 : value.shape[0], :] = value.astype(F32)


def down_rows(flags, res, wd_ref, bd_ref, height):
    half = (res.shape[1] - 8) // 2
    band = flags[2]
    rows = []
    for i in range(height // 2):
        cols = [
            res[2 * i + a + band, pl.ds(b, half, stride=2), :].astype(BF16)
            for a in range(3)
            for b in range(3)
        ]
        rows.append(jnp.concatenate(cols, axis=1))
    out = jnp.dot(jnp.concatenate(rows, axis=0), wd_ref[...], preferred_element_type=F32)
    out = (out + bd_ref[...]).astype(BF16)
    return out.reshape(height // 2, half, -1)


def out_row(flags, i, rows):
    return jnp.where(flags[2] == 0, rows - 1 - i, i)


def second_kernel(cells, flags, b1, b2, eb_ref, tp_ref, a1, a2, e_ref, t_ref, g_ref, c_ref, w_ref, in_ref, bias_ref, own, mate, eo_ref, em_ref, wd_ref, bd_ref, acc_ref, out_ref, stack, res):
    out_rows, width, channels = acc_ref.shape
    height = out_rows - 1
    even = flags[0] == 0
    params = norm_params(jnp.where(flags[1] == 1, t_ref[0], tp_ref[1]), g_ref[...], c_ref[...], cells)
    values = [
        either(flags, f, o) for f, o in zip(halves(e_ref, 0, a1, a2), halves(eb_ref, 0, b1, b2))
    ]
    fill_frame(stack, values, params)
    close_stack(stack)
    res[:, width:, :] = jnp.zeros((res.shape[0], res.shape[1] - width, channels), F32)
    res[out_rows] = jnp.zeros(res.shape[1:], F32)
    for start, count in steps(0, out_rows):
        part = taps(stack, w_ref[...], start, count).reshape(count, width, 2 * channels)
        branch = in_ref[start : start + count] + part + bias_ref[...]
        acc_ref[start : start + count] = branch[:, :, :channels]
        for k in range(count):
            r = start + k - 1
            raw = jnp.where(even, mate[r], own[r]) if r >= 0 else jnp.where(even, em_ref[0], eo_ref[0])
            put_row(res, r + 1, residual_row(raw, branch[k, :, channels:]))
    out = down_rows(flags, res, wd_ref, bd_ref, height)
    for i in range(height // 2):
        out_ref[out_row(flags, i, height // 2)] = out[i]


def first_near_kernel(cells, flags, p1, ep_ref, tp_ref, a1, e_ref, t_ref, g_ref, c_ref, w_ref, in_ref, own, mate, eo_ref, em_ref, out_ref, stack):
    rows, width, channels = out_ref.shape
    even = flags[0] == 0
    params = norm_params(jnp.where(flags[1] == 1, t_ref[0], tp_ref[0]), g_ref[...], c_ref[...], cells)
    firsts = [lambda: e_ref[0, 1], lambda: e_ref[0, 0]] + [reader(a1, r) for r in range(rows)]
    others = [lambda: ep_ref[0, 1], lambda: ep_ref[0, 0]] + [reader(p1, r) for r in range(rows)]
    fill_frame(stack, [either(flags, f, o) for f, o in zip(firsts, others)], params)
    for start, count in steps(0, rows):
        part = taps(stack, w_ref[...], start, count).reshape(count, width, channels)
        branch = in_ref[start : start + count] + part
        for k in range(count):
            r = start + k - 1
            raw = jnp.where(even, own[r], mate[r]) if r >= 0 else jnp.where(even, eo_ref[0], em_ref[0])
            out_ref[r + 1] = residual_row(raw, branch[k])


def first_far_kernel(cells, flags, p1, p2, tp_ref, a1, a2, t_ref, g_ref, c_ref, w_ref, in_ref, near_ref, other_ref, own, mate, wd_ref, bd_ref, send_ref, keep_ref, stack, res):
    out_rows, width, channels = in_ref.shape
    height = out_rows - 1
    half = p1.shape[0]
    done = near_ref.shape[0]
    even = flags[0] == 0
    params = norm_params(jnp.where(flags[1] == 1, t_ref[0], tp_ref[0]), g_ref[...], c_ref[...], cells)
    values = []
    for r in range(done - 2, height):
        f, o, k = (a1, p1, r) if r < half else (a2, p2, r - half)
        values.append(either(flags, reader(f, k), reader(o, k)))
    fill_frame(stack, values, params)
    close_stack(stack)
    res[:, width:, :] = jnp.zeros((res.shape[0], res.shape[1] - width, channels), F32)
    res[out_rows] = jnp.zeros(res.shape[1:], F32)
    for r in range(done):
        put_row(res, r, near_ref[r])
    for start, count in steps(0, out_rows - done):
        part = taps(stack, w_ref[...], start, count).reshape(count, width, channels)
        branch = in_ref[done + start : done + start + count] + part
        for k in range(count):
            r = done + start + k - 1
            put_row(res, r + 1, residual_row(jnp.where(even, own[r], mate[r]), branch[k]))
    out = down_rows(flags, res, wd_ref, bd_ref, height)
    for i in range(height // 2):
        row = out_row(flags, i, height // 2)
        other = other_ref[row]
        send_ref[row] = jnp.where(even, other, out[i])
        keep_ref[row] = jnp.where(even, out[i], other)


def call(kernel, out_shape, scratch, flags, *args, aliases=None, flops=0):
    vmem = pl.BlockSpec(memory_space=pltpu.VMEM)
    several = isinstance(out_shape, (list, tuple))
    moved = sum(a.size * a.dtype.itemsize for a in args)
    return pl.pallas_call(
        kernel,
        out_shape=out_shape,
        in_specs=[pl.BlockSpec(memory_space=pltpu.SMEM)] + [vmem] * len(args),
        out_specs=[vmem] * len(out_shape) if several else vmem,
        scratch_shapes=scratch,
        input_output_aliases=aliases or {},
        cost_estimate=pl.CostEstimate(flops=flops, bytes_accessed=moved, transcendentals=0),
        compiler_params=pltpu.CompilerParams(vmem_limit_bytes=32 << 20),
    )(flags, *args)


def slot_weights(kernel, band):
    channels = kernel.shape[-1]
    kernel = jnp.where(band == 0, kernel[::-1], kernel)
    by_frame = jnp.transpose(kernel, (2, 0, 1, 3, 4)).reshape(3, -1, channels)
    padded = jnp.pad(by_frame, ((1, 1), (0, 0), (0, 0)))
    return jnp.concatenate([padded[1:], padded[:-1]], axis=-1)


def local(
    frames_in,
    gain_one,
    norm_bias_one,
    kernel_one,
    bias_one,
    gain_two,
    norm_bias_two,
    kernel_two,
    bias_two,
    kernel_down,
    bias_down,
):
    x = frames_in[:, 0]
    clips, height, width, channels = x.shape
    count = lax.axis_size("tm")
    bands = lax.axis_size("rows")
    assert clips == 2 and bands == 2 and count % 2 == 0 and height % 4 == 0
    cells = height * bands * width
    near = height // 2
    position = lax.axis_index("tm")
    band = lax.axis_index("rows")
    side = position % 2
    even = side == 0
    flags = jnp.stack([side, (position < 2).astype(jnp.int32), band]).astype(jnp.int32)
    swap = [(i, i ^ 1) for i in range(count)]
    onward = [(i, (i + 2) % count) for i in range(count)]
    across = [(0, 1), (1, 0)]

    def swapped(v):
        return lax.ppermute(v, "tm", swap)

    def later(v):
        return lax.ppermute(v, "tm", onward)

    def beside(v):
        return lax.ppermute(v, "rows", across)

    def pick(pair, index):
        return lax.dynamic_index_in_dim(pair, index, 0, keepdims=False)

    def row(v):
        return v.reshape(1, -1)

    def stack(rows):
        return pltpu.VMEM((rows, width, 3 * channels), BF16)

    def flops(rows, slots):
        return 2 * rows * width * 9 * channels * 2 * channels * slots

    def shape(*dims, dtype=BF16):
        return jax.ShapeDtypeStruct(dims, dtype)

    def kernel(body, *rest, **options):
        return call(functools.partial(body, cells), *rest, **options)

    frame = (height, width, channels)
    own, other = call(place_kernel, [shape(*frame), shape(*frame)], [], flags, x)
    own_before = later(own)
    mate = swapped(other)
    partial = call_sums(x)
    totals = partial + beside(partial)
    own_total = pick(totals, side)
    mate_total = swapped(pick(totals, 1 - side))
    both_before = later(jnp.stack([own_total, mate_total]))
    own_edge = beside(own[:1])

    weights = slot_weights(kernel_one, band)
    norm_one = (row(gain_one), row(norm_bias_one))
    acc = kernel(
        own_kernel,
        shape(height, width, 2 * channels, dtype=F32),
        [stack(height + 2)],
        flags,
        own,
        own_edge,
        own_total,
        *norm_one,
        pick(weights, 2 + side),
        flops=flops(height, 1),
    )

    before_near = later(mate[: near + 1])
    before_far = later(mate[near + 1 :])
    mate_edge = beside(mate[:1])
    own_before_edge = beside(own_before[:1])
    acc = kernel(
        mates_kernel,
        shape(height, width, 2 * channels, dtype=F32),
        [stack(height + 2), stack(height + 2)],
        flags,
        mate,
        mate_edge,
        mate_total,
        own_before,
        own_before_edge,
        both_before[0],
        own,
        own_edge,
        own_total,
        *norm_one,
        pick(weights, 3 - side),
        pick(weights, side),
        acc,
        flops=flops(height, 2),
    )
    before_edge = beside(before_near[:1])
    last = pick(weights, 1 - side)
    bias = row(jnp.tile(bias_one, 2))
    part = shape(near, width, channels)
    sums = shape(2, 8, channels, dtype=F32)
    a1, b1, edges, sums_near = kernel(
        near_kernel,
        [part, part, shape(2, 2, width, channels), sums],
        [stack(near + 2)],
        flags,
        before_near,
        before_edge,
        both_before[1],
        own,
        own_edge,
        own_total,
        mate,
        mate_edge,
        mate_total,
        *norm_one,
        last,
        acc,
        bias,
        flops=flops(near, 1),
    )
    b1_before = later(b1)
    a2, b2, sums_far = kernel(
        far_kernel,
        [part, part, sums],
        [stack(near + 2)],
        flags,
        before_near,
        before_far,
        both_before[1],
        own,
        own_total,
        mate,
        mate_total,
        *norm_one,
        last,
        acc,
        bias,
        flops=flops(near, 1),
    )
    b2_before = later(b2)
    partial = sums_near + sums_far
    totals = partial + beside(partial)
    totals_before = later(totals)
    a1_before = later(a1)
    a2_before = later(a2)
    edges = beside(edges)

    weights = slot_weights(kernel_two, band)
    norm_two = (row(gain_two), row(norm_bias_two))
    acc = kernel(
        local_kernel,
        shape(height + 1, width, 2 * channels, dtype=F32),
        [stack(height + 3), stack(height + 3)],
        flags,
        a1,
        a2,
        b1,
        b2,
        edges,
        totals,
        *norm_two,
        weights[2],
        weights[3],
        flops=flops(height + 1, 2),
    )
    down = jnp.where(band == 0, kernel_down[::-1], kernel_down).reshape(-1, channels)
    residual = pltpu.VMEM((height + 2, width + 8, channels), F32)
    out_shape = shape(height // 2, width // 2, channels)
    b_edge = beside(b1_before[None, :2])
    acc, out_b = kernel(
        second_kernel,
        [shape(height + 1, width, channels, dtype=F32), out_shape],
        [stack(height + 3), residual],
        flags,
        b1_before,
        b2_before,
        b_edge,
        totals_before,
        a1,
        a2,
        edges,
        totals,
        *norm_two,
        weights[1],
        acc,
        row(jnp.tile(bias_two, 2)),
        own,
        mate,
        own_edge,
        mate_edge,
        down,
        row(bias_down),
        flops=flops(height + 1, 1),
    )
    a_edge = beside(a1_before[None, :2])
    thin = weights[0][:, :channels]
    first_near = kernel(
        first_near_kernel,
        part,
        [stack(near + 2)],
        flags,
        a1_before,
        a_edge,
        totals_before,
        a1,
        edges,
        totals,
        *norm_two,
        thin,
        acc,
        own,
        mate,
        own_edge,
        mate_edge,
        flops=flops(near, 1),
    )
    sent, kept = kernel(
        first_far_kernel,
        [out_shape, out_shape],
        [stack(near + 3), residual],
        flags,
        a1_before,
        a2_before,
        totals_before,
        a1,
        a2,
        totals,
        *norm_two,
        thin,
        acc,
        first_near,
        out_b,
        own,
        mate,
        down,
        row(bias_down),
        flops=flops(near, 1),
    )
    received = swapped(sent)
    result = jnp.where(even, jnp.stack([kept, received]), jnp.stack([received, kept]))
    return result[:, None]


def call_sums(x):
    clips, _, _, channels = x.shape
    vmem = pl.BlockSpec(memory_space=pltpu.VMEM)
    return pl.pallas_call(
        sums_kernel,
        out_shape=jax.ShapeDtypeStruct((clips, 8, channels), F32),
        in_specs=[vmem],
        out_specs=vmem,
        cost_estimate=pl.CostEstimate(flops=4 * x.size, bytes_accessed=2 * x.size, transcendentals=0),
    )(x)


def solution(mesh):
    placed = (P("groups", "tm", "rows", None, None),) + (P(),) * 10
    return jax.shard_map(
        local,
        mesh=mesh,
        in_specs=placed,
        out_specs=P("groups", "tm", "rows", None, None),
        check_vma=False,
    )
```

```python
import functools

import jax
import jax.numpy as jnp
from jax import lax
from jax.experimental import pallas as pl
from jax.experimental.pallas import tpu as pltpu
from jax.sharding import PartitionSpec as P


G = 32
EPSILON = 1e-06
F32 = jnp.float32
BF16 = jnp.bfloat16


def norm_params(totals, gain, bias, cells):
    channels = totals.shape[1]
    size = channels // G
    left = lax.broadcasted_iota(jnp.int32, (channels, channels), 0) // size
    right = lax.broadcasted_iota(jnp.int32, (channels, channels), 1) // size
    same = (left == right).astype(F32)
    grouped = jnp.dot(totals, same, precision=lax.Precision.HIGHEST, preferred_element_type=F32)
    grouped = grouped / (cells * size)
    mean = grouped[0:1]
    inverse = lax.rsqrt(grouped[1:2] - mean * mean + EPSILON)
    return mean, inverse * gain, bias


def keep_params(ref, params):
    for k, value in enumerate(params):
        ref[k : k + 1] = value


def kept_params(ref):
    return ref[0:1], ref[1:2], ref[2:3]


def clear_line(line):
    edge = jnp.zeros((line.shape[0], 8, line.shape[2]), F32)
    line[:, 0:8] = edge
    line[:, line.shape[1] - 8 :] = edge


def fill_row(stack, line, r, values, params):
    mean, scale, bias = params
    width, channels = values.shape
    half = 0.5 * ((values.astype(F32) - mean) * scale + bias)
    normed = half + half * jnp.tanh(half)
    k = r % line.shape[0]
    line[k, 8 : 8 + width] = normed
    stack[r, :, 0:channels] = line[k, 7 : 7 + width].astype(BF16)
    stack[r, :, channels : 2 * channels] = normed.astype(BF16)
    stack[r, :, 2 * channels :] = line[k, 9 : 9 + width].astype(BF16)


def fill_frame(stack, line, values, params):
    for r, value in enumerate(values):
        fill_row(stack, line, r, value(), params)


def close_stack(stack):
    last = stack.shape[0] - 1
    stack[last] = jnp.zeros(stack.shape[1:], BF16)


def taps(stack, weights, start, count):
    rows = [
        jnp.concatenate([stack[r], stack[r + 1], stack[r + 2]], axis=1)
        for r in range(start, start + count)
    ]
    return jnp.dot(jnp.concatenate(rows, axis=0), weights, preferred_element_type=F32)


def steps(first, last):
    total = last - first
    size = 3 if total % 3 == 0 else 2
    return [(r, min(size, last - r)) for r in range(first, last, size)]


def reader(ref, r):
    return lambda: ref[r]


def choose(flags, r, part, k, own, mate):
    def read():
        return jnp.where(flags[1] == 1, jnp.where(flags[0] == 0, own[r], mate[r]), part[k])

    return read


def place_kernel(flags, x_ref, own_ref, other_ref, sem):
    height = own_ref.shape[0]
    side, band = flags[0], flags[2]
    copies = []
    for k, (clip, ref) in enumerate(((side, own_ref), (1 - side, other_ref))):
        for r in range(height):
            row = jnp.where(band == 0, height - 1 - r, r)
            copies.append(pltpu.make_async_copy(x_ref.at[clip, row], ref.at[r], sem.at[k, r]))
    for copy in copies:
        copy.start()
    for copy in copies:
        copy.wait()


def weights_kernel(slots, flags, *refs):
    k_ref, *outs = refs
    channels = k_ref.shape[-1]
    band = flags[2]
    for slot, out in zip(slots(flags), outs):
        for f in range(out.shape[1] // channels):
            frame = slot - f
            known = jnp.logical_and(frame >= 0, frame <= 2)
            frame = jnp.clip(frame, 0, 2)
            for a in range(3):
                tap = jnp.where(band == 0, 2 - a, a)
                for b in range(3):
                    k = (3 * a + b) * channels
                    block = jnp.where(known, k_ref[tap, b, frame], jnp.zeros((), BF16))
                    out[k : k + channels, f * channels : (f + 1) * channels] = block


def sums_kernel(own_ref, other_ref, out_ref):
    height, width, channels = own_ref.shape
    for c, x_ref in enumerate((own_ref, other_ref)):
        total = jnp.zeros((8, channels), F32)
        square = jnp.zeros((8, channels), F32)
        for r in range(height):
            v = x_ref[r].astype(F32).reshape(width // 8, 8, channels)
            total += jnp.sum(v, axis=0)
            square += jnp.sum(v * v, axis=0)
        out_ref[c, 0:1] = jnp.sum(total, axis=0, keepdims=True)
        out_ref[c, 1:2] = jnp.sum(square, axis=0, keepdims=True)
        out_ref[c, 2:8] = jnp.zeros((6, channels), F32)


def own_kernel(cells, flags, x_ref, e_ref, t_ref, g_ref, c_ref, w_ref, acc_ref, stack, line):
    height, width, _ = x_ref.shape
    clear_line(line)
    params = norm_params(t_ref[...], g_ref[...], c_ref[...], cells)
    fill_frame(stack, line, [reader(e_ref, 0)] + [reader(x_ref, r) for r in range(height)], params)
    close_stack(stack)
    for start, count in steps(0, height):
        part = taps(stack, w_ref[...], start, count)
        acc_ref[start : start + count] = part.reshape(count, width, -1)


def mates_kernel(cells, flags, m_ref, tm_ref, p_ref, e_ref, tp_ref, o_ref, eo_ref, to_ref, tq_ref, g_ref, c_ref, wm_ref, wp_ref, in_ref, acc_ref, last_ref, xm, xp, line):
    height, width, _ = m_ref.shape
    first, even = flags[1] == 1, flags[0] == 0
    clear_line(line)
    params = norm_params(tm_ref[...], g_ref[...], c_ref[...], cells)
    fill_frame(xm, line, [reader(e_ref, 0)] + [reader(m_ref, r) for r in range(height)], params)
    close_stack(xm)
    start_totals = jnp.where(even, to_ref[...], tm_ref[...])
    totals = jnp.where(first, start_totals, tp_ref[...])
    params = norm_params(totals, g_ref[...], c_ref[...], cells)
    values = [lambda: jnp.where(first, jnp.where(even, eo_ref[0], e_ref[0]), e_ref[1])]
    values += [choose(flags, r, p_ref, r, o_ref, m_ref) for r in range(height)]
    fill_frame(xp, line, values, params)
    close_stack(xp)
    for start, count in steps(0, height):
        part = taps(xm, wm_ref[...], start, count) + taps(xp, wp_ref[...], start, count)
        acc_ref[start : start + count] = in_ref[start : start + count] + part.reshape(count, width, -1)
    totals = jnp.where(first, start_totals, tq_ref[...])
    keep_params(last_ref, norm_params(totals, g_ref[...], c_ref[...], cells))


def hidden_rows(stack, w_ref, in_ref, bias_ref, first, a_ref, b_ref, sum_ref):
    rows, width, channels = a_ref.shape
    both = 2 * channels
    total = jnp.zeros((8, both), F32)
    square = jnp.zeros((8, both), F32)
    for start, count in steps(0, rows):
        part = taps(stack, w_ref[...], start, count).reshape(count, width, both)
        begin = first + start
        hidden = (in_ref[begin : begin + count] + part + bias_ref[...]).astype(BF16)
        a_ref[start : start + count] = hidden[:, :, :channels]
        b_ref[start : start + count] = hidden[:, :, channels:]
        wide = hidden.astype(F32).reshape(count * width // 8, 8, both)
        total += jnp.sum(wide, axis=0)
        square += jnp.sum(wide * wide, axis=0)
    total = jnp.sum(total, axis=0, keepdims=True)
    square = jnp.sum(square, axis=0, keepdims=True)
    for k in range(2):
        sum_ref[k, 0:1] = total[:, k * channels : (k + 1) * channels]
        sum_ref[k, 1:2] = square[:, k * channels : (k + 1) * channels]
        sum_ref[k, 2:8] = jnp.zeros((6, channels), F32)


def near_kernel(cells, flags, p_ref, ep_ref, n_ref, o_ref, eo_ref, m_ref, e_ref, w_ref, in_ref, bias_ref, a_ref, b_ref, edge_ref, sum_ref, stack, line):
    clear_line(line)
    rows = a_ref.shape[0]
    values = [choose(flags, 0, ep_ref, 0, eo_ref, e_ref)]
    values += [choose(flags, r, p_ref, r, o_ref, m_ref) for r in range(rows + 1)]
    fill_frame(stack, line, values, kept_params(n_ref))
    hidden_rows(stack, w_ref, in_ref, bias_ref, 0, a_ref, b_ref, sum_ref)
    edge_ref[0] = a_ref[0:2]
    edge_ref[1] = b_ref[0:2]


def far_kernel(cells, flags, p_ref, q_ref, n_ref, o_ref, m_ref, w_ref, in_ref, bias_ref, near_ref, part_ref, a_ref, b_ref, c_ref, sum_ref, stack, line, held):
    clear_line(line)
    height, near = o_ref.shape[0], p_ref.shape[0]
    rows, early = b_ref.shape[0], near_ref.shape[0]
    values = []
    for r in range(height - rows - 1, height):
        part, k = (p_ref, r) if r < near else (q_ref, r - near)
        values.append(choose(flags, r, part, k, o_ref, m_ref))
    fill_frame(stack, line, values, kept_params(n_ref))
    close_stack(stack)
    hidden_rows(stack, w_ref, in_ref, bias_ref, height - rows, held, b_ref, sum_ref)
    sum_ref[...] += part_ref[...]
    whole = a_ref.shape[0]
    a_ref[0:early] = near_ref[...]
    a_ref[early:] = held[0 : whole - early]
    c_ref[...] = held[whole - early :]


def halves(edge, k, near, far):
    rows = [lambda: edge[k, 1], lambda: edge[k, 0]]
    rows += [reader(near, r) for r in range(near.shape[0])]
    return rows + [reader(far, r) for r in range(far.shape[0])]


def local_kernel(cells, flags, a1, a2, b1, b2, e_ref, t_ref, g_ref, c_ref, wa_ref, wb_ref, acc_ref, xa, xb, line):
    out_rows, width, _ = acc_ref.shape
    clear_line(line)
    for k, (stack, near, far) in enumerate(((xa, a1, a2), (xb, b1, b2))):
        params = norm_params(t_ref[k], g_ref[...], c_ref[...], cells)
        fill_frame(stack, line, halves(e_ref, k, near, far), params)
        close_stack(stack)
    for start, count in steps(0, out_rows):
        part = taps(xa, wa_ref[...], start, count) + taps(xb, wb_ref[...], start, count)
        acc_ref[start : start + count] = part.reshape(count, width, -1)


def either(flags, first, other):
    return lambda: jnp.where(flags[1] == 1, first(), other())


def residual_row(raw, branch):
    return (raw.astype(F32) + branch).astype(BF16)


def put_row(res, r, value):
    res[r, 0 : value.shape[0], :] = value.astype(F32)


def down_rows(flags, res, wd_ref, bd_ref, first, last):
    half = (res.shape[1] - 8) // 2
    band = flags[2]
    rows = []
    for i in range(first, last):
        cols = [
            res[2 * i + a + band, pl.ds(b, half, stride=2), :].astype(BF16)
            for a in range(3)
            for b in range(3)
        ]
        rows.append(jnp.concatenate(cols, axis=1))
    out = jnp.dot(jnp.concatenate(rows, axis=0), wd_ref[...], preferred_element_type=F32)
    out = (out + bd_ref[...]).astype(BF16)
    return out.reshape(last - first, half, -1)


def second_kernel(cells, flags, b1, b2, eb_ref, tp_ref, a1, a2, e_ref, t_ref, g_ref, c_ref, w_ref, in_ref, bias_ref, own, mate, eo_ref, em_ref, wd_ref, bd_ref, acc_ref, out_ref, last_ref, stack, line, res):
    out_rows, width, channels = acc_ref.shape
    height = out_rows - 1
    even = flags[0] == 0
    clear_line(line)
    params = norm_params(jnp.where(flags[1] == 1, t_ref[0], tp_ref[1]), g_ref[...], c_ref[...], cells)
    values = [
        either(flags, f, o) for f, o in zip(halves(e_ref, 0, a1, a2), halves(eb_ref, 0, b1, b2))
    ]
    fill_frame(stack, line, values, params)
    close_stack(stack)
    res[:, width:, :] = jnp.zeros((res.shape[0], res.shape[1] - width, channels), F32)
    res[out_rows] = jnp.zeros(res.shape[1:], F32)
    for start, count in steps(0, out_rows):
        part = taps(stack, w_ref[...], start, count).reshape(count, width, 2 * channels)
        branch = in_ref[start : start + count] + part + bias_ref[...]
        acc_ref[start : start + count] = branch[:, :, :channels]
        for k in range(count):
            r = start + k - 1
            raw = jnp.where(even, mate[r], own[r]) if r >= 0 else jnp.where(even, em_ref[0], eo_ref[0])
            put_row(res, r + 1, residual_row(raw, branch[k, :, channels:]))
    out_ref[...] = down_rows(flags, res, wd_ref, bd_ref, 0, height // 2)
    params = norm_params(jnp.where(flags[1] == 1, t_ref[0], tp_ref[0]), g_ref[...], c_ref[...], cells)
    keep_params(last_ref, params)


def route(flags, out, other_ref, first, send_ref, keep_ref):
    even = flags[0] == 0
    other = other_ref[first : first + out.shape[0]]
    send_ref[...] = jnp.where(even, other, out)
    keep_ref[...] = jnp.where(even, out, other)


def first_near_kernel(cells, flags, p1, ep_ref, n_ref, a1, e_ref, w_ref, in_ref, own, mate, eo_ref, em_ref, other_ref, wd_ref, bd_ref, out_ref, send_ref, keep_ref, stack, line, res):
    rows, width, channels = out_ref.shape
    even = flags[0] == 0
    clear_line(line)
    firsts = [lambda: e_ref[0, 1], lambda: e_ref[0, 0]] + [reader(a1, r) for r in range(rows)]
    others = [lambda: ep_ref[0, 1], lambda: ep_ref[0, 0]] + [reader(p1, r) for r in range(rows)]
    values = [either(flags, f, o) for f, o in zip(firsts, others)]
    fill_frame(stack, line, values, kept_params(n_ref))
    res[:, width:, :] = jnp.zeros((res.shape[0], res.shape[1] - width, channels), F32)
    for start, count in steps(0, rows):
        part = taps(stack, w_ref[...], start, count).reshape(count, width, channels)
        branch = in_ref[start : start + count] + part
        for k in range(count):
            r = start + k - 1
            raw = jnp.where(even, own[r], mate[r]) if r >= 0 else jnp.where(even, eo_ref[0], em_ref[0])
            value = residual_row(raw, branch[k])
            out_ref[r + 1] = value
            put_row(res, r + 1, value)
    out = down_rows(flags, res, wd_ref, bd_ref, 0, send_ref.shape[0])
    route(flags, out, other_ref, 0, send_ref, keep_ref)


def first_far_kernel(cells, flags, p1, p2, n_ref, a1, a2, w_ref, in_ref, near_ref, other_ref, own, mate, wd_ref, bd_ref, send_ref, keep_ref, stack, line, res):
    out_rows, width, channels = in_ref.shape
    height = out_rows - 1
    half = p1.shape[0]
    done = near_ref.shape[0]
    even = flags[0] == 0
    clear_line(line)
    values = []
    for r in range(done - 2, height):
        f, o, k = (a1, p1, r) if r < half else (a2, p2, r - half)
        values.append(either(flags, reader(f, k), reader(o, k)))
    fill_frame(stack, line, values, kept_params(n_ref))
    close_stack(stack)
    first = height // 2 - send_ref.shape[0]
    res[:, width:, :] = jnp.zeros((res.shape[0], res.shape[1] - width, channels), F32)
    res[out_rows] = jnp.zeros(res.shape[1:], F32)
    for r in range(2 * first, done):
        put_row(res, r, near_ref[r])
    for start, count in steps(0, out_rows - done):
        part = taps(stack, w_ref[...], start, count).reshape(count, width, channels)
        branch = in_ref[done + start : done + start + count] + part
        for k in range(count):
            r = done + start + k - 1
            put_row(res, r + 1, residual_row(jnp.where(even, own[r], mate[r]), branch[k]))
    out = down_rows(flags, res, wd_ref, bd_ref, first, height // 2)
    route(flags, out, other_ref, first, send_ref, keep_ref)


def join_kernel(flags, kept1, kept2, got1, got2, out_ref):
    rows = out_ref.shape[1]
    for clip, parts in ((flags[0], (kept1, kept2)), (1 - flags[0], (got1, got2))):
        for i in range(rows):
            part, k = (parts[0], i) if i < kept1.shape[0] else (parts[1], i - kept1.shape[0])
            out_ref[clip, jnp.where(flags[2] == 0, rows - 1 - i, i)] = part[k]


def call(kernel, out_shape, scratch, flags, *args, flops=0):
    vmem = pl.BlockSpec(memory_space=pltpu.VMEM)
    several = isinstance(out_shape, (list, tuple))
    moved = sum(a.size * a.dtype.itemsize for a in args)
    return pl.pallas_call(
        kernel,
        out_shape=out_shape,
        in_specs=[pl.BlockSpec(memory_space=pltpu.SMEM)] + [vmem] * len(args),
        out_specs=[vmem] * len(out_shape) if several else vmem,
        scratch_shapes=scratch,
        cost_estimate=pl.CostEstimate(flops=flops, bytes_accessed=moved, transcendentals=0),
        compiler_params=pltpu.CompilerParams(vmem_limit_bytes=32 << 20),
    )(flags, *args)


def call_place(flags, x, frame):
    height = frame.shape[0]
    vmem = pl.BlockSpec(memory_space=pltpu.VMEM)
    return pl.pallas_call(
        place_kernel,
        out_shape=[frame, frame],
        in_specs=[pl.BlockSpec(memory_space=pltpu.SMEM), pl.BlockSpec(memory_space=pl.ANY)],
        out_specs=[vmem, vmem],
        scratch_shapes=[pltpu.SemaphoreType.DMA((2, height))],
        cost_estimate=pl.CostEstimate(flops=0, bytes_accessed=4 * x.size, transcendentals=0),
    )(flags, x)


def call_sums(own, other):
    channels = own.shape[-1]
    vmem = pl.BlockSpec(memory_space=pltpu.VMEM)
    return pl.pallas_call(
        sums_kernel,
        out_shape=jax.ShapeDtypeStruct((2, 8, channels), F32),
        in_specs=[vmem, vmem],
        out_specs=vmem,
        cost_estimate=pl.CostEstimate(flops=8 * own.size, bytes_accessed=4 * own.size, transcendentals=0),
    )(own, other)


def slots_one(flags):
    side = flags[0]
    return 2 + side, 3 - side, side, 1 - side


def slots_two(flags):
    return 2, 3, 1, 0


def turned(value, band):
    return jnp.where(band == 0, value[::-1], value)


def local(
    frames_in,
    gain_one,
    norm_bias_one,
    kernel_one,
    bias_one,
    gain_two,
    norm_bias_two,
    kernel_two,
    bias_two,
    kernel_down,
    bias_down,
):
    x = frames_in[:, 0]
    clips, height, width, channels = x.shape
    count = lax.axis_size("tm")
    bands = lax.axis_size("rows")
    assert clips == 2 and bands == 2 and count % 2 == 0 and height % 8 == 0
    cells = height * bands * width
    near = 3 * height // 8
    tail = height // TAIL
    position = lax.axis_index("tm")
    band = lax.axis_index("rows")
    side = position % 2
    flags = jnp.stack([side, (position < 2).astype(jnp.int32), band]).astype(jnp.int32)
    swap = [(i, i ^ 1) for i in range(count)]
    across = [(0, 1), (1, 0)]

    def onward(name, turn):
        wrap = name not in OPEN
        pairs = [(i, (i ^ turn) + 2) for i in range(count)]
        return [(i, j % count) for i, j in pairs if wrap or j < count]

    def swapped(v):
        return lax.ppermute(v, "tm", swap)

    def later(v, name):
        return lax.ppermute(v, "tm", onward(name, 0))

    def crossed(v, name):
        return lax.ppermute(v, "tm", onward(name, 1))

    def beside(v):
        return lax.ppermute(v, "rows", across)

    def row(v):
        return v.reshape(1, -1)

    def stack(rows):
        line = pltpu.VMEM((2, width + 16, channels), F32)
        return [pltpu.VMEM((rows, width, 3 * channels), BF16), line]

    def flops(rows, slots):
        return 2 * rows * width * 9 * channels * 2 * channels * slots

    def shape(*dims, dtype=BF16):
        return jax.ShapeDtypeStruct(dims, dtype)

    def kernel(body, *rest, **options):
        return call(functools.partial(body, cells), *rest, **options)

    def weights(slots, kernel, last):
        shapes = [shape(9 * channels, n * channels) for n in (2, 2, 2, last)]
        return call(functools.partial(weights_kernel, slots), shapes, [], flags, kernel)

    own, other = call_place(flags, x, shape(height, width, channels))
    own_on = later(own, "own_on")
    mate = swapped(other)
    partial = call_sums(own, other)
    totals = partial + beside(partial)
    own_total, other_total = totals[0], totals[1]
    own_on_total = later(own_total, "own_sums")
    cross_total = crossed(other_total, "cross_sums")
    mate_total = swapped(other_total)
    own_edge = beside(own[:1])
    split = near + 1
    cross_near = crossed(other[:split], "cross1")
    cross_far = crossed(other[split:], "cross2")

    w_own, w_mate, w_own_on, w_cross = weights(slots_one, kernel_one, 2)
    norm_one = (row(gain_one), row(norm_bias_one))
    sums = shape(2, 8, channels, dtype=F32)
    params = shape(8, channels, dtype=F32)
    acc_shape = shape(height, width, 2 * channels, dtype=F32)
    acc = kernel(
        own_kernel,
        acc_shape,
        stack(height + 2),
        flags,
        own,
        own_edge,
        own_total,
        *norm_one,
        w_own,
        flops=flops(height, 1),
    )
    pair_edge = beside(jnp.concatenate([mate[:1], own_on[:1]]))
    acc, cross_params = kernel(
        mates_kernel,
        [acc_shape, params],
        stack(height + 2)[:1] + stack(height + 2),
        flags,
        mate,
        mate_total,
        own_on,
        pair_edge,
        own_on_total,
        own,
        own_edge,
        own_total,
        cross_total,
        *norm_one,
        w_mate,
        w_own_on,
        acc,
        flops=flops(height, 2),
    )
    cross_edge = beside(cross_near[:1])
    bias = row(jnp.tile(bias_one, 2))
    part = shape(near, width, channels)
    rest = shape(height - near, width, channels)
    early = shape(height - tail, width, channels)
    a_near, b1, edges, sums_near = kernel(
        near_kernel,
        [part, part, shape(2, 2, width, channels), sums],
        stack(near + 2),
        flags,
        cross_near,
        cross_edge,
        cross_params,
        own,
        own_edge,
        mate,
        pair_edge,
        w_cross,
        acc,
        bias,
        flops=flops(near, 1),
    )
    b1_on = later(b1, "b_on1")
    a1, b2, a2, partial = kernel(
        far_kernel,
        [early, rest, shape(tail, width, channels), sums],
        stack(height - near + 2) + [pltpu.VMEM(rest.shape, BF16)],
        flags,
        cross_near,
        cross_far,
        cross_params,
        own,
        mate,
        w_cross,
        acc,
        bias,
        a_near,
        sums_near,
        flops=flops(height - near, 1),
    )
    b2_on = later(b2, "b_on2")
    totals = partial + beside(partial)
    totals_on = later(totals, "hsums_on")
    a1_on = later(a1, "a_on1")
    a2_on = later(a2, "a_on2")
    edges = beside(edges)

    w_a, w_b, w_b_on, w_a_on = weights(slots_two, kernel_two, 1)
    norm_two = (row(gain_two), row(norm_bias_two))
    acc = kernel(
        local_kernel,
        shape(height + 1, width, 2 * channels, dtype=F32),
        stack(height + 3)[:1] + stack(height + 3),
        flags,
        a1,
        a2,
        b1,
        b2,
        edges,
        totals,
        *norm_two,
        w_a,
        w_b,
        flops=flops(height + 1, 2),
    )
    down = turned(kernel_down, band).reshape(-1, channels)
    residual = [pltpu.VMEM((height + 2, width + 8, channels), F32)]
    b_edge = beside(b1_on[None, :2])
    acc, out_b, a_params = kernel(
        second_kernel,
        [
            shape(height + 1, width, channels, dtype=F32),
            shape(height // 2, width // 2, channels),
            params,
        ],
        stack(height + 3) + residual,
        flags,
        b1_on,
        b2_on,
        b_edge,
        totals_on,
        a1,
        a2,
        edges,
        totals,
        *norm_two,
        w_b_on,
        acc,
        row(jnp.tile(bias_two, 2)),
        own,
        mate,
        own_edge,
        pair_edge,
        down,
        row(bias_down),
        flops=flops(height + 1, 1),
    )
    a_edge = beside(a1_on[None, :2])
    ready = height - tail
    early_out = (ready - 2) // 2
    late_out = height // 2 - early_out
    half_out = shape(early_out, width // 2, channels)
    last_out = shape(late_out, width // 2, channels)
    first_near, sent1, kept1 = kernel(
        first_near_kernel,
        [shape(ready, width, channels), half_out, half_out],
        stack(ready + 2) + residual,
        flags,
        a1_on,
        a_edge,
        a_params,
        a1,
        edges,
        w_a_on,
        acc,
        own,
        mate,
        own_edge,
        pair_edge,
        out_b,
        down,
        row(bias_down),
        flops=flops(ready, 1),
    )
    got1 = swapped(sent1)
    sent2, kept2 = kernel(
        first_far_kernel,
        [last_out, last_out],
        stack(tail + 3) + residual,
        flags,
        a1_on,
        a2_on,
        a_params,
        a1,
        a2,
        w_a_on,
        acc,
        first_near,
        out_b,
        own,
        mate,
        down,
        row(bias_down),
        flops=flops(tail + 1, 1),
    )
    got2 = swapped(sent2)
    result = call(
        join_kernel,
        shape(2, height // 2, width // 2, channels),
        [],
        flags,
        kept1,
        kept2,
        got1,
        got2,
    )
    return result[:, None]


OPEN = ()
TAIL = 2


def solution(mesh):
    placed = (P("groups", "tm", "rows", None, None),) + (P(),) * 10
    return jax.shard_map(
        local,
        mesh=mesh,
        in_specs=placed,
        out_specs=P("groups", "tm", "rows", None, None),
        check_vma=False,
    )
```

```python
import functools

import jax
import jax.numpy as jnp
from jax import lax
from jax.experimental import pallas as pl
from jax.experimental.pallas import tpu as pltpu
from jax.sharding import PartitionSpec as P


G = 32
EPSILON = 1e-06
F32 = jnp.float32
VMEM_LIMIT = 16 << 20
BF16 = jnp.bfloat16


def norm_params(totals, gain, bias, cells):
    channels = totals.shape[1]
    size = channels // G
    left = lax.broadcasted_iota(jnp.int32, (channels, channels), 0) // size
    right = lax.broadcasted_iota(jnp.int32, (channels, channels), 1) // size
    same = (left == right).astype(F32)
    grouped = jnp.dot(totals, same, precision=lax.Precision.HIGHEST, preferred_element_type=F32)
    grouped = grouped / (cells * size)
    mean = grouped[0:1]
    inverse = lax.rsqrt(grouped[1:2] - mean * mean + EPSILON)
    return mean, inverse * gain, bias


def keep_params(ref, params):
    for k, value in enumerate(params):
        ref[k : k + 1] = value


def kept_params(ref):
    return ref[0:1], ref[1:2], ref[2:3]


def fill_row(stack, r, values, params):
    mean, scale, bias = params
    width, channels = values.shape
    half = 0.5 * ((values.astype(F32) - mean) * scale + bias)
    normed = half + half * jnp.tanh(half)
    column = lax.broadcasted_iota(jnp.int32, (width, channels), 0)
    before = jnp.where(column == 0, 0.0, pltpu.roll(normed, 1, 0))
    after = jnp.where(column == width - 1, 0.0, pltpu.roll(normed, width - 1, 0))
    stack[r, :, 0:channels] = before.astype(BF16)
    stack[r, :, channels : 2 * channels] = normed.astype(BF16)
    stack[r, :, 2 * channels :] = after.astype(BF16)


def fill_frame(stack, values, params):
    for r, value in enumerate(values):
        fill_row(stack, r, value(), params)


def close_stack(stack):
    last = stack.shape[0] - 1
    stack[last] = jnp.zeros(stack.shape[1:], BF16)


def taps(stack, weights, start, count):
    rows = [
        jnp.concatenate([stack[r], stack[r + 1], stack[r + 2]], axis=1)
        for r in range(start, start + count)
    ]
    return jnp.dot(jnp.concatenate(rows, axis=0), weights, preferred_element_type=F32)


def steps(first, last):
    total = last - first
    size = 3 if total % 3 == 0 else 2
    return [(r, min(size, last - r)) for r in range(first, last, size)]


def reader(ref, r):
    return lambda: ref[r]


def rows_of(*refs):
    return [reader(ref, r) for ref in refs for r in range(ref.shape[0])]


def choose(flags, part, own, mate):
    def read():
        return jnp.where(flags[1] == 1, jnp.where(flags[0] == 0, own(), mate()), part())

    return read


def chosen(flags, parts, owns, mates):
    return [choose(flags, p, o, m) for p, o, m in zip(parts, owns, mates)]


def place_kernel(flags, x_ref, *parts):
    height = x_ref.shape[1]
    side, band = flags[0], flags[2]
    clips = [side] * height + [1 - side] * height
    rows = list(range(height)) * 2
    for part in parts:
        for k in range(part.shape[0]):
            r = rows.pop(0)
            part[k] = x_ref[clips.pop(0), jnp.where(band == 0, height - 1 - r, r)]


def lay_weights(out, k_ref, slot, band):
    channels = k_ref.shape[-1]
    for f in range(out.shape[1] // channels):
        frame = slot - f
        known = jnp.logical_and(frame >= 0, frame <= 2)
        frame = jnp.clip(frame, 0, 2)
        for a in range(3):
            tap = jnp.where(band == 0, 2 - a, a)
            for b in range(3):
                k = (3 * a + b) * channels
                block = jnp.where(known, k_ref[tap, b, frame], jnp.zeros((), BF16))
                out[k : k + channels, f * channels : (f + 1) * channels] = block


def sums_kernel(flags, own, other, out_ref):
    width, channels = own[0].shape[1:]
    for c, rows in enumerate((rows_of(*own), rows_of(*other))):
        total = jnp.zeros((8, channels), F32)
        square = jnp.zeros((8, channels), F32)
        for read in rows:
            v = read().astype(F32).reshape(width // 8, 8, channels)
            total += jnp.sum(v, axis=0)
            square += jnp.sum(v * v, axis=0)
        out_ref[c, 0:1] = jnp.sum(total, axis=0, keepdims=True)
        out_ref[c, 1:2] = jnp.sum(square, axis=0, keepdims=True)
        out_ref[c, 2:8] = jnp.zeros((6, channels), F32)


def own_kernel(cells, flags, own, t_ref, g_ref, c_ref, k_ref, acc_ref, stack, w_ref):
    height, width, _ = acc_ref.shape
    lay_weights(w_ref, k_ref, 2 + flags[0], flags[2])
    params = norm_params(t_ref[0], g_ref[...], c_ref[...], cells)
    fill_frame(stack, rows_of(*own), params)
    close_stack(stack)
    for start, count in steps(0, height):
        part = taps(stack, w_ref[...], start, count)
        acc_ref[start : start + count] = part.reshape(count, width, -1)


def mates_kernel(cells, flags, own, mate, past, to_ref, tm_ref, tp_ref, tq_ref, g_ref, c_ref, k_ref, in_ref, acc_ref, last_ref, edge_ref, xm, xp, wm, wp):
    height, width, _ = acc_ref.shape
    side = flags[0]
    first, even = flags[1] == 1, side == 0
    lay_weights(wm, k_ref, 3 - side, flags[2])
    lay_weights(wp, k_ref, side, flags[2])
    params = norm_params(tm_ref[1], g_ref[...], c_ref[...], cells)
    fill_frame(xm, rows_of(*mate), params)
    close_stack(xm)
    start_totals = jnp.where(even, to_ref[0], tm_ref[1])
    totals = jnp.where(first, start_totals, tp_ref[0])
    params = norm_params(totals, g_ref[...], c_ref[...], cells)
    fill_frame(xp, chosen(flags, rows_of(*past), rows_of(*own), rows_of(*mate)), params)
    close_stack(xp)
    for start, count in steps(0, height):
        part = taps(xm, wm[...], start, count) + taps(xp, wp[...], start, count)
        acc_ref[start : start + count] = in_ref[start : start + count] + part.reshape(count, width, -1)
    totals = jnp.where(first, start_totals, tq_ref[1])
    keep_params(last_ref, norm_params(totals, g_ref[...], c_ref[...], cells))
    edge_ref[0] = own[0][0]
    edge_ref[1] = mate[0][0]


def hidden_rows(stack, w_ref, in_ref, bias_ref, first, a_ref, b_ref, sum_ref):
    rows, width, channels = a_ref.shape
    both = 2 * channels
    bias = jnp.concatenate([bias_ref[...], bias_ref[...]], axis=1)
    total = jnp.zeros((8, both), F32)
    square = jnp.zeros((8, both), F32)
    for start, count in steps(0, rows):
        part = taps(stack, w_ref[...], start, count).reshape(count, width, both)
        begin = first + start
        hidden = (in_ref[begin : begin + count] + part + bias).astype(BF16)
        a_ref[start : start + count] = hidden[:, :, :channels]
        b_ref[start : start + count] = hidden[:, :, channels:]
        wide = hidden.astype(F32).reshape(count * width // 8, 8, both)
        total += jnp.sum(wide, axis=0)
        square += jnp.sum(wide * wide, axis=0)
    total = jnp.sum(total, axis=0, keepdims=True)
    square = jnp.sum(square, axis=0, keepdims=True)
    for k in range(2):
        sum_ref[k, 0:1] = total[:, k * channels : (k + 1) * channels]
        sum_ref[k, 1:2] = square[:, k * channels : (k + 1) * channels]
        sum_ref[k, 2:8] = jnp.zeros((6, channels), F32)


def near_kernel(cells, flags, own, mate, past, n_ref, k_ref, in_ref, bias_ref, a_ref, b_ref, edge_ref, sum_ref, stack, w_ref):
    lay_weights(w_ref, k_ref, 1 - flags[0], flags[2])
    edges = own[0]
    owns = [reader(edges, 0)] + rows_of(*own[1:])
    mates = [reader(edges, 1)] + rows_of(*mate)
    fill_frame(stack, chosen(flags, rows_of(*past), owns, mates), kept_params(n_ref))
    hidden_rows(stack, w_ref, in_ref, bias_ref, 0, a_ref, b_ref, sum_ref)
    edge_ref[0] = a_ref[0:2]
    edge_ref[1] = b_ref[0:2]


def far_kernel(cells, flags, own, mate, past, n_ref, k_ref, in_ref, bias_ref, near_ref, part_ref, a_ref, b_ref, c_ref, sum_ref, stack, held, w_ref):
    lay_weights(w_ref, k_ref, 1 - flags[0], flags[2])
    height = in_ref.shape[0]
    rows, early = b_ref.shape[0], near_ref.shape[0]
    values = chosen(flags, rows_of(*past), rows_of(*own), rows_of(*mate))
    fill_frame(stack, values[height - rows - 1 :], kept_params(n_ref))
    close_stack(stack)
    hidden_rows(stack, w_ref, in_ref, bias_ref, height - rows, held, b_ref, sum_ref)
    sum_ref[...] += part_ref[...]
    whole = a_ref.shape[0]
    a_ref[0:early] = near_ref[...]
    a_ref[early:] = held[0 : whole - early]
    c_ref[...] = held[whole - early :]


def halves(edge, k, near, far):
    return [lambda: edge[k, 1], lambda: edge[k, 0]] + rows_of(near, far)


def local_kernel(cells, flags, a1, a2, b1, b2, e_ref, t_ref, g_ref, c_ref, k_ref, acc_ref, xa, xb, wa, wb):
    out_rows, width, _ = acc_ref.shape
    lay_weights(wa, k_ref, 2, flags[2])
    lay_weights(wb, k_ref, 3, flags[2])
    for k, (stack, near, far) in enumerate(((xa, a1, a2), (xb, b1, b2))):
        params = norm_params(t_ref[k], g_ref[...], c_ref[...], cells)
        fill_frame(stack, halves(e_ref, k, near, far), params)
        close_stack(stack)
    for start, count in steps(0, out_rows):
        part = taps(xa, wa[...], start, count) + taps(xb, wb[...], start, count)
        acc_ref[start : start + count] = part.reshape(count, width, -1)


def either(flags, first, other):
    return lambda: jnp.where(flags[1] == 1, first(), other())


def residual_row(raw, branch):
    return (raw.astype(F32) + branch).astype(BF16)


def put_row(res, r, value):
    res[r, 0 : value.shape[0], :] = value.astype(F32)


def down_rows(flags, res, wd_ref, bd_ref, first, last):
    half = (res.shape[1] - 8) // 2
    band = flags[2]
    rows = []
    for i in range(first, last):
        cols = [
            res[2 * i + a + band, pl.ds(b, half, stride=2), :].astype(BF16)
            for a in range(3)
            for b in range(3)
        ]
        rows.append(jnp.concatenate(cols, axis=1))
    out = jnp.dot(jnp.concatenate(rows, axis=0), wd_ref[...], preferred_element_type=F32)
    out = (out + bd_ref[...]).astype(BF16)
    return out.reshape(last - first, half, -1)


def raw_rows(even, first, second):
    return [lambda f=f, s=s: jnp.where(even, f(), s()) for f, s in zip(first, second)]


def second_kernel(cells, flags, b1, b2, eb_ref, tp_ref, a1, a2, e_ref, t_ref, g_ref, c_ref, k_ref, in_ref, bias_ref, own, mate, wd_ref, bd_ref, acc_ref, out_ref, last_ref, wl_ref, stack, res, w_ref):
    out_rows, width, channels = acc_ref.shape
    height = out_rows - 1
    lay_weights(w_ref, k_ref, 1, flags[2])
    lay_weights(wl_ref, k_ref, 0, flags[2])
    params = norm_params(jnp.where(flags[1] == 1, t_ref[0], tp_ref[1]), g_ref[...], c_ref[...], cells)
    values = [
        either(flags, f, o) for f, o in zip(halves(e_ref, 0, a1, a2), halves(eb_ref, 0, b1, b2))
    ]
    fill_frame(stack, values, params)
    close_stack(stack)
    raw = raw_rows(flags[0] == 0, rows_of(*mate), rows_of(*own))
    bias = jnp.concatenate([bias_ref[...], bias_ref[...]], axis=1)
    res[:, width:, :] = jnp.zeros((res.shape[0], res.shape[1] - width, channels), F32)
    res[out_rows] = jnp.zeros(res.shape[1:], F32)
    for start, count in steps(0, out_rows):
        part = taps(stack, w_ref[...], start, count).reshape(count, width, 2 * channels)
        branch = in_ref[start : start + count] + part + bias
        acc_ref[start : start + count] = branch[:, :, :channels]
        for k in range(count):
            put_row(res, start + k, residual_row(raw[start + k](), branch[k, :, channels:]))
    out_ref[...] = down_rows(flags, res, wd_ref, bd_ref, 0, height // 2)
    params = norm_params(jnp.where(flags[1] == 1, t_ref[0], tp_ref[0]), g_ref[...], c_ref[...], cells)
    keep_params(last_ref, params)


def first_near_kernel(cells, flags, p1, ep_ref, n_ref, a1, e_ref, w_ref, in_ref, own, mate, out_ref, stack):
    rows, width, channels = out_ref.shape
    firsts = [lambda: e_ref[0, 1], lambda: e_ref[0, 0]] + rows_of(a1)
    others = [lambda: ep_ref[0, 1], lambda: ep_ref[0, 0]] + rows_of(p1)
    fill_frame(stack, [either(flags, f, o) for f, o in zip(firsts, others)], kept_params(n_ref))
    raw = raw_rows(flags[0] == 0, rows_of(*own), rows_of(*mate))
    for start, count in steps(0, rows):
        part = taps(stack, w_ref[...], start, count).reshape(count, width, channels)
        branch = in_ref[start : start + count] + part
        for k in range(count):
            out_ref[start + k] = residual_row(raw[start + k](), branch[k])


def first_far_kernel(cells, flags, p1, p2, n_ref, a1, a2, w_ref, in_ref, near_ref, other_ref, own, mate, wd_ref, bd_ref, send_ref, keep_ref, stack, res):
    out_rows, width, channels = in_ref.shape
    height = out_rows - 1
    done = near_ref.shape[0]
    even = flags[0] == 0
    values = [either(flags, f, o) for f, o in zip(rows_of(a1, a2), rows_of(p1, p2))]
    fill_frame(stack, values[done - 2 :], kept_params(n_ref))
    close_stack(stack)
    raw = raw_rows(even, rows_of(*own), rows_of(*mate))
    res[:, width:, :] = jnp.zeros((res.shape[0], res.shape[1] - width, channels), F32)
    res[out_rows] = jnp.zeros(res.shape[1:], F32)
    for r in range(done):
        put_row(res, r, near_ref[r])
    for start, count in steps(0, out_rows - done):
        part = taps(stack, w_ref[...], start, count).reshape(count, width, channels)
        branch = in_ref[done + start : done + start + count] + part
        for k in range(count):
            r = done + start + k
            put_row(res, r, residual_row(raw[r - 1](), branch[k]))
    out = down_rows(flags, res, wd_ref, bd_ref, 0, height // 2)
    rows = height // 2
    for i in range(rows):
        row = jnp.where(flags[2] == 0, rows - 1 - i, i)
        send_ref[row] = jnp.where(even, other_ref[i], out[i])
        keep_ref[row] = jnp.where(even, out[i], other_ref[i])


def call(body, out_shape, scratch, flags, *groups, flops=0):
    vmem = pl.BlockSpec(memory_space=pltpu.VMEM)
    several = isinstance(out_shape, (list, tuple))
    args = [a for g in groups for a in (g if isinstance(g, tuple) else (g,))]
    moved = sum(a.size * a.dtype.itemsize for a in args)

    def kernel(flags_ref, *refs):
        rest = list(refs)
        given = [
            tuple(rest.pop(0) for _ in g) if isinstance(g, tuple) else rest.pop(0) for g in groups
        ]
        body(flags_ref, *given, *rest)

    return pl.pallas_call(
        kernel,
        out_shape=out_shape,
        in_specs=[pl.BlockSpec(memory_space=pltpu.SMEM)] + [vmem] * len(args),
        out_specs=[vmem] * len(out_shape) if several else vmem,
        scratch_shapes=scratch,
        cost_estimate=pl.CostEstimate(flops=flops, bytes_accessed=moved, transcendentals=0),
        compiler_params=pltpu.CompilerParams(vmem_limit_bytes=VMEM_LIMIT),
    )(flags, *args)


def turned(value, band):
    return jnp.where(band == 0, value[::-1], value)


def local(
    frames_in,
    gain_one,
    norm_bias_one,
    kernel_one,
    bias_one,
    gain_two,
    norm_bias_two,
    kernel_two,
    bias_two,
    kernel_down,
    bias_down,
):
    x = frames_in[:, 0]
    clips, height, width, channels = x.shape
    count = lax.axis_size("tm")
    bands = lax.axis_size("rows")
    assert clips == 2 and bands == 2 and count % 2 == 0 and height % 8 == 0
    cells = height * bands * width
    near = 3 * height // 8
    tail = height // TAIL
    position = lax.axis_index("tm")
    band = lax.axis_index("rows")
    side = position % 2
    flags = jnp.stack([side, (position < 2).astype(jnp.int32), band]).astype(jnp.int32)
    swap = [(i, i ^ 1) for i in range(count)]
    across = [(0, 1), (1, 0)]

    def onward(name, turn):
        wrap = name not in OPEN
        pairs = [(i, (i ^ turn) + 2) for i in range(count)]
        return [(i, j % count) for i, j in pairs if wrap or j < count]

    def swapped(v):
        return lax.ppermute(v, "tm", swap)

    def later(v, name):
        return lax.ppermute(v, "tm", onward(name, 0))

    def crossed(v, name):
        return lax.ppermute(v, "tm", onward(name, 1))

    def beside(v):
        return lax.ppermute(v, "rows", across)

    def row(v):
        return v.reshape(1, -1)

    def stack(rows):
        return [pltpu.VMEM((rows, width, 3 * channels), BF16)]

    def laid(n):
        return [pltpu.VMEM((9 * channels, n * channels), BF16)]

    def flops(rows, slots):
        return 2 * rows * width * 9 * channels * 2 * channels * slots

    def shape(*dims, dtype=BF16):
        return jax.ShapeDtypeStruct(dims, dtype)

    def kernel(body, *rest, **options):
        return call(functools.partial(body, cells), *rest, **options)

    split = near + 1
    sizes = (1, height - 1, 1, split - 1, height - split)
    parts = call(place_kernel, [shape(n, width, channels) for n in sizes], [], flags, x)
    own, other = tuple(parts[:2]), tuple(parts[2:])
    past = later(own[0], "own_on0"), later(own[1], "own_on1")
    mate = tuple(swapped(v) for v in other)
    partial = call(sums_kernel, shape(2, 8, channels, dtype=F32), [], flags, own, other)
    totals = partial + beside(partial)
    own_on_total = later(totals, "own_sums")
    cross_total = crossed(totals, "cross_sums")
    mate_total = swapped(totals)
    own = (beside(own[0]), *own)
    mate_on = tuple(later(v, f"mate_on{k}") for k, v in enumerate(mate))
    mate = (beside(mate[0]), *mate)
    past = (beside(past[0]), *past)

    norm_one = (row(gain_one), row(norm_bias_one))
    sums = shape(2, 8, channels, dtype=F32)
    params = shape(8, channels, dtype=F32)
    acc_shape = shape(height, width, 2 * channels, dtype=F32)
    acc = kernel(
        own_kernel,
        acc_shape,
        stack(height + 2) + laid(2),
        flags,
        own,
        totals,
        *norm_one,
        kernel_one,
        flops=flops(height, 1),
    )
    acc, cross_params, fall_edges = kernel(
        mates_kernel,
        [acc_shape, params, shape(2, width, channels)],
        stack(height + 2) + stack(height + 2) + laid(2) + laid(2),
        flags,
        own,
        mate,
        past,
        totals,
        mate_total,
        own_on_total,
        cross_total,
        *norm_one,
        kernel_one,
        acc,
        flops=flops(height, 2),
    )
    cross_edge = beside(mate_on[0])
    bias = row(bias_one)
    part = shape(near, width, channels)
    rest = shape(height - near, width, channels)
    early = shape(height - tail, width, channels)
    a_near, b1, edges, sums_near = kernel(
        near_kernel,
        [part, part, shape(2, 2, width, channels), sums],
        stack(near + 2) + laid(2),
        flags,
        (fall_edges, *own[1:]),
        mate[1:3],
        (cross_edge, *mate_on[:2]),
        cross_params,
        kernel_one,
        acc,
        bias,
        flops=flops(near, 1),
    )
    b1_on = later(b1, "b_on1")
    a1, b2, a2, partial = kernel(
        far_kernel,
        [early, rest, shape(tail, width, channels), sums],
        stack(height - near + 2) + [pltpu.VMEM(rest.shape, BF16)] + laid(2),
        flags,
        own[1:],
        mate[1:],
        mate_on,
        cross_params,
        kernel_one,
        acc,
        bias,
        a_near,
        sums_near,
        flops=flops(height - near, 1),
    )
    b2_on = later(b2, "b_on2")
    totals = partial + beside(partial)
    totals_on = later(totals, "hsums_on")
    a1_on = later(a1, "a_on1")
    a2_on = later(a2, "a_on2")
    edges = beside(edges)

    norm_two = (row(gain_two), row(norm_bias_two))
    acc = kernel(
        local_kernel,
        shape(height + 1, width, 2 * channels, dtype=F32),
        stack(height + 3) + stack(height + 3) + laid(2) + laid(2),
        flags,
        a1,
        a2,
        b1,
        b2,
        edges,
        totals,
        *norm_two,
        kernel_two,
        flops=flops(height + 1, 2),
    )
    down = turned(kernel_down, band).reshape(-1, channels)
    residual = [pltpu.VMEM((height + 2, width + 8, channels), F32)]
    b_edge = beside(b1_on[None, :2])
    out_shape = shape(height // 2, width // 2, channels)
    acc, out_b, a_params, w_a_on = kernel(
        second_kernel,
        [shape(height + 1, width, channels, dtype=F32), out_shape, params, shape(9 * channels, channels)],
        stack(height + 3) + residual + laid(2),
        flags,
        b1_on,
        b2_on,
        b_edge,
        totals_on,
        a1,
        a2,
        edges,
        totals,
        *norm_two,
        kernel_two,
        acc,
        row(bias_two),
        own,
        mate,
        down,
        row(bias_down),
        flops=flops(height + 1, 1),
    )
    a_edge = beside(a1_on[None, :2])
    ready = height - tail
    first_near = kernel(
        first_near_kernel,
        shape(ready, width, channels),
        stack(ready + 2),
        flags,
        a1_on,
        a_edge,
        a_params,
        a1,
        edges,
        w_a_on,
        acc,
        own,
        mate[:3],
        flops=flops(ready, 1),
    )
    sent, kept = kernel(
        first_far_kernel,
        [out_shape, out_shape],
        stack(tail + 3) + residual,
        flags,
        a1_on,
        a2_on,
        a_params,
        a1,
        a2,
        w_a_on,
        acc,
        first_near,
        out_b,
        own[1:],
        mate[1:],
        down,
        row(bias_down),
        flops=flops(tail + 1, 1),
    )
    received = swapped(sent)
    even = side == 0
    result = jnp.where(even, jnp.stack([kept, received]), jnp.stack([received, kept]))
    return result[:, None]


OPEN = ('b_on1', 'b_on2', 'a_on1', 'a_on2', 'hsums_on')
TAIL = 2


def solution(mesh):
    placed = (P("groups", "tm", "rows", None, None),) + (P(),) * 10
    return jax.shard_map(
        local,
        mesh=mesh,
        in_specs=placed,
        out_specs=P("groups", "tm", "rows", None, None),
        check_vma=False,
    )
```

```python
import functools

import jax
import jax.numpy as jnp
from jax import lax
from jax.experimental import pallas as pl
from jax.experimental.pallas import tpu as pltpu
from jax.sharding import PartitionSpec as P


G = 32
EPSILON = 1e-06
F32 = jnp.float32
VMEM_LIMIT = 16 << 20
BF16 = jnp.bfloat16


def norm_params(totals, gain, bias, cells):
    channels = totals.shape[1]
    size = channels // G
    left = lax.broadcasted_iota(jnp.int32, (channels, channels), 0) // size
    right = lax.broadcasted_iota(jnp.int32, (channels, channels), 1) // size
    same = (left == right).astype(F32)
    grouped = jnp.dot(totals, same, precision=lax.Precision.HIGHEST, preferred_element_type=F32)
    grouped = grouped / (cells * size)
    mean = grouped[0:1]
    inverse = lax.rsqrt(grouped[1:2] - mean * mean + EPSILON)
    return mean, inverse * gain, bias


def keep_params(ref, params):
    for k, value in enumerate(params):
        ref[k : k + 1] = value


def kept_params(ref):
    return ref[0:1], ref[1:2], ref[2:3]


def fill_row(stack, r, values, params):
    mean, scale, bias = params
    width, channels = values.shape
    half = 0.5 * ((values.astype(F32) - mean) * scale + bias)
    normed = half + half * jnp.tanh(half)
    column = lax.broadcasted_iota(jnp.int32, (width, channels), 0)
    before = jnp.where(column == 0, 0.0, pltpu.roll(normed, 1, 0))
    after = jnp.where(column == width - 1, 0.0, pltpu.roll(normed, width - 1, 0))
    stack[r, :, 0:channels] = before.astype(BF16)
    stack[r, :, channels : 2 * channels] = normed.astype(BF16)
    stack[r, :, 2 * channels :] = after.astype(BF16)


def taps(stack, weights, start, count):
    rows = [
        jnp.concatenate([stack[r], stack[r + 1], stack[r + 2]], axis=1)
        for r in range(start, start + count)
    ]
    return jnp.dot(jnp.concatenate(rows, axis=0), weights, preferred_element_type=F32)


def steps(first, last):
    total = last - first
    size = 3 if total % 3 == 0 else 2
    return [(r, min(size, last - r)) for r in range(first, last, size)]


def sweep(frames, first, last, emit):
    filled = 0

    def fill(until):
        nonlocal filled
        for r in range(filled, until):
            for stack, values, params, _ in frames:
                if r < len(values):
                    fill_row(stack, r, values[r](), params)
                else:
                    stack[r] = jnp.zeros(stack.shape[1:], BF16)
        filled = max(filled, until)

    groups = steps(first, last)
    fill(sum(groups[0]) + 2)
    for k, (start, count) in enumerate(groups):
        part = sum(taps(stack, weights[...], start, count) for stack, _, _, weights in frames)
        if k + 1 < len(groups):
            fill(sum(groups[k + 1]) + 2)
        emit(start, count, part)


def reader(ref, r):
    return lambda: ref[r]


def rows_of(*refs):
    return [reader(ref, r) for ref in refs for r in range(ref.shape[0])]


def choose(flags, part, own, mate):
    def read():
        return jnp.where(flags[1] == 1, jnp.where(flags[0] == 0, own(), mate()), part())

    return read


def chosen(flags, parts, owns, mates):
    return [choose(flags, p, o, m) for p, o, m in zip(parts, owns, mates)]


def place_kernel(flags, x_ref, *parts):
    height = x_ref.shape[1]
    side, band = flags[0], flags[2]
    clips = [side] * height + [1 - side] * height
    rows = list(range(height)) * 2
    for part in parts:
        for k in range(part.shape[0]):
            r = rows.pop(0)
            part[k] = x_ref[clips.pop(0), jnp.where(band == 0, height - 1 - r, r)]


def lay_weights(out, k_ref, slot, band):
    channels = k_ref.shape[-1]
    for f in range(out.shape[1] // channels):
        frame = slot - f
        known = jnp.logical_and(frame >= 0, frame <= 2)
        frame = jnp.clip(frame, 0, 2)
        for a in range(3):
            tap = jnp.where(band == 0, 2 - a, a)
            for b in range(3):
                k = (3 * a + b) * channels
                block = jnp.where(known, k_ref[tap, b, frame], jnp.zeros((), BF16))
                out[k : k + channels, f * channels : (f + 1) * channels] = block


def sums_kernel(flags, own, other, out_ref):
    width, channels = own[0].shape[1:]
    for c, rows in enumerate((rows_of(*own), rows_of(*other))):
        total = jnp.zeros((8, channels), F32)
        square = jnp.zeros((8, channels), F32)
        for read in rows:
            v = read().astype(F32).reshape(width // 8, 8, channels)
            total += jnp.sum(v, axis=0)
            square += jnp.sum(v * v, axis=0)
        out_ref[c, 0:1] = jnp.sum(total, axis=0, keepdims=True)
        out_ref[c, 1:2] = jnp.sum(square, axis=0, keepdims=True)
        out_ref[c, 2:8] = jnp.zeros((6, channels), F32)


def own_kernel(cells, flags, own, t_ref, g_ref, c_ref, k_ref, acc_ref, stack, w_ref):
    height, width, _ = acc_ref.shape
    lay_weights(w_ref, k_ref, 2 + flags[0], flags[2])
    params = norm_params(t_ref[0], g_ref[...], c_ref[...], cells)

    def emit(start, count, part):
        acc_ref[start : start + count] = part.reshape(count, width, -1)

    sweep([(stack, rows_of(*own), params, w_ref)], 0, height, emit)


def mates_kernel(cells, flags, own, mate, past, to_ref, tm_ref, tp_ref, tq_ref, g_ref, c_ref, k_ref, in_ref, acc_ref, last_ref, edge_ref, xm, xp, wm, wp):
    height, width, _ = acc_ref.shape
    side = flags[0]
    first, even = flags[1] == 1, side == 0
    lay_weights(wm, k_ref, 3 - side, flags[2])
    lay_weights(wp, k_ref, side, flags[2])
    params = norm_params(tm_ref[1], g_ref[...], c_ref[...], cells)
    frames = [(xm, rows_of(*mate), params, wm)]
    start_totals = jnp.where(even, to_ref[0], tm_ref[1])
    totals = jnp.where(first, start_totals, tp_ref[0])
    params = norm_params(totals, g_ref[...], c_ref[...], cells)
    values = chosen(flags, rows_of(*past), rows_of(*own), rows_of(*mate))
    frames.append((xp, values, params, wp))

    def emit(start, count, part):
        acc_ref[start : start + count] = in_ref[start : start + count] + part.reshape(count, width, -1)

    sweep(frames, 0, height, emit)
    totals = jnp.where(first, start_totals, tq_ref[1])
    keep_params(last_ref, norm_params(totals, g_ref[...], c_ref[...], cells))
    edge_ref[0] = own[0][0]
    edge_ref[1] = mate[0][0]


def hidden_rows(stack, values, params, w_ref, in_ref, bias_ref, first, a_ref, b_ref, sum_ref):
    rows, width, channels = a_ref.shape
    both = 2 * channels
    bias = jnp.concatenate([bias_ref[...], bias_ref[...]], axis=1)
    total = jnp.zeros((8, both), F32)
    square = jnp.zeros((8, both), F32)

    def emit(start, count, part):
        nonlocal total, square
        begin = first + start
        part = part.reshape(count, width, both)
        hidden = (in_ref[begin : begin + count] + part + bias).astype(BF16)
        a_ref[start : start + count] = hidden[:, :, :channels]
        b_ref[start : start + count] = hidden[:, :, channels:]
        wide = hidden.astype(F32).reshape(count * width // 8, 8, both)
        total += jnp.sum(wide, axis=0)
        square += jnp.sum(wide * wide, axis=0)

    sweep([(stack, values, params, w_ref)], 0, rows, emit)
    total = jnp.sum(total, axis=0, keepdims=True)
    square = jnp.sum(square, axis=0, keepdims=True)
    for k in range(2):
        sum_ref[k, 0:1] = total[:, k * channels : (k + 1) * channels]
        sum_ref[k, 1:2] = square[:, k * channels : (k + 1) * channels]
        sum_ref[k, 2:8] = jnp.zeros((6, channels), F32)


def near_kernel(cells, flags, own, mate, past, n_ref, k_ref, in_ref, bias_ref, a_ref, b_ref, edge_ref, sum_ref, stack, w_ref):
    lay_weights(w_ref, k_ref, 1 - flags[0], flags[2])
    edges = own[0]
    owns = [reader(edges, 0)] + rows_of(*own[1:])
    mates = [reader(edges, 1)] + rows_of(*mate)
    values = chosen(flags, rows_of(*past), owns, mates)
    hidden_rows(stack, values, kept_params(n_ref), w_ref, in_ref, bias_ref, 0, a_ref, b_ref, sum_ref)
    edge_ref[0] = a_ref[0:2]
    edge_ref[1] = b_ref[0:2]


def far_kernel(cells, flags, own, mate, past, n_ref, k_ref, in_ref, bias_ref, near_ref, part_ref, a_ref, b_ref, c_ref, sum_ref, stack, held, w_ref):
    lay_weights(w_ref, k_ref, 1 - flags[0], flags[2])
    height = in_ref.shape[0]
    rows, early = b_ref.shape[0], near_ref.shape[0]
    values = chosen(flags, rows_of(*past), rows_of(*own), rows_of(*mate))
    first = height - rows
    hidden_rows(stack, values[first - 1 :], kept_params(n_ref), w_ref, in_ref, bias_ref, first, held, b_ref, sum_ref)
    sum_ref[...] += part_ref[...]
    whole = a_ref.shape[0]
    a_ref[0:early] = near_ref[...]
    a_ref[early:] = held[0 : whole - early]
    c_ref[...] = held[whole - early :]


def halves(edge, k, near, far):
    return [lambda: edge[k, 1], lambda: edge[k, 0]] + rows_of(near, far)


def local_kernel(cells, flags, a1, a2, b1, b2, e_ref, t_ref, g_ref, c_ref, k_ref, acc_ref, xa, xb, wa, wb):
    out_rows, width, _ = acc_ref.shape
    lay_weights(wa, k_ref, 2, flags[2])
    lay_weights(wb, k_ref, 3, flags[2])
    frames = []
    for k, (stack, near, far, weights) in enumerate(((xa, a1, a2, wa), (xb, b1, b2, wb))):
        params = norm_params(t_ref[k], g_ref[...], c_ref[...], cells)
        frames.append((stack, halves(e_ref, k, near, far), params, weights))

    def emit(start, count, part):
        acc_ref[start : start + count] = part.reshape(count, width, -1)

    sweep(frames, 0, out_rows, emit)


def either(flags, first, other):
    return lambda: jnp.where(flags[1] == 1, first(), other())


def residual_row(raw, branch):
    return (raw.astype(F32) + branch).astype(BF16)


def put_row(res, r, value):
    res[r, 0 : value.shape[0], :] = value.astype(F32)


def down_rows(flags, res, wd_ref, bd_ref, first, last):
    half = (res.shape[1] - 8) // 2
    band = flags[2]
    rows = []
    for i in range(first, last):
        cols = [
            res[2 * i + a + band, pl.ds(b, half, stride=2), :].astype(BF16)
            for a in range(3)
            for b in range(3)
        ]
        rows.append(jnp.concatenate(cols, axis=1))
    out = jnp.dot(jnp.concatenate(rows, axis=0), wd_ref[...], preferred_element_type=F32)
    out = (out + bd_ref[...]).astype(BF16)
    return out.reshape(last - first, half, -1)


def raw_rows(even, first, second):
    return [lambda f=f, s=s: jnp.where(even, f(), s()) for f, s in zip(first, second)]


def second_kernel(cells, flags, b1, b2, eb_ref, tp_ref, a1, a2, e_ref, t_ref, g_ref, c_ref, k_ref, in_ref, bias_ref, own, mate, wd_ref, bd_ref, acc_ref, out_ref, last_ref, wl_ref, stack, res, w_ref):
    out_rows, width, channels = acc_ref.shape
    height = out_rows - 1
    lay_weights(w_ref, k_ref, 1, flags[2])
    lay_weights(wl_ref, k_ref, 0, flags[2])
    params = norm_params(jnp.where(flags[1] == 1, t_ref[0], tp_ref[1]), g_ref[...], c_ref[...], cells)
    values = [
        either(flags, f, o) for f, o in zip(halves(e_ref, 0, a1, a2), halves(eb_ref, 0, b1, b2))
    ]
    raw = raw_rows(flags[0] == 0, rows_of(*mate), rows_of(*own))
    bias = jnp.concatenate([bias_ref[...], bias_ref[...]], axis=1)
    res[:, width:, :] = jnp.zeros((res.shape[0], res.shape[1] - width, channels), F32)
    res[out_rows] = jnp.zeros(res.shape[1:], F32)

    def emit(start, count, part):
        part = part.reshape(count, width, 2 * channels)
        branch = in_ref[start : start + count] + part + bias
        acc_ref[start : start + count] = branch[:, :, :channels]
        for k in range(count):
            put_row(res, start + k, residual_row(raw[start + k](), branch[k, :, channels:]))

    sweep([(stack, values, params, w_ref)], 0, out_rows, emit)
    out_ref[...] = down_rows(flags, res, wd_ref, bd_ref, 0, height // 2)
    params = norm_params(jnp.where(flags[1] == 1, t_ref[0], tp_ref[0]), g_ref[...], c_ref[...], cells)
    keep_params(last_ref, params)


def first_near_kernel(cells, flags, p1, ep_ref, n_ref, a1, e_ref, w_ref, in_ref, own, mate, out_ref, stack):
    rows, width, channels = out_ref.shape
    firsts = [lambda: e_ref[0, 1], lambda: e_ref[0, 0]] + rows_of(a1)
    others = [lambda: ep_ref[0, 1], lambda: ep_ref[0, 0]] + rows_of(p1)
    values = [either(flags, f, o) for f, o in zip(firsts, others)]
    raw = raw_rows(flags[0] == 0, rows_of(*own), rows_of(*mate))

    def emit(start, count, part):
        branch = in_ref[start : start + count] + part.reshape(count, width, channels)
        for k in range(count):
            out_ref[start + k] = residual_row(raw[start + k](), branch[k])

    sweep([(stack, values, kept_params(n_ref), w_ref)], 0, rows, emit)


def first_far_kernel(cells, flags, p1, p2, n_ref, a1, a2, w_ref, in_ref, near_ref, other_ref, own, mate, wd_ref, bd_ref, send_ref, keep_ref, stack, res):
    out_rows, width, channels = in_ref.shape
    height = out_rows - 1
    done = near_ref.shape[0]
    even = flags[0] == 0
    values = [either(flags, f, o) for f, o in zip(rows_of(a1, a2), rows_of(p1, p2))]
    raw = raw_rows(even, rows_of(*own), rows_of(*mate))
    res[:, width:, :] = jnp.zeros((res.shape[0], res.shape[1] - width, channels), F32)
    res[out_rows] = jnp.zeros(res.shape[1:], F32)
    for r in range(done):
        put_row(res, r, near_ref[r])

    def emit(start, count, part):
        begin = done + start
        branch = in_ref[begin : begin + count] + part.reshape(count, width, channels)
        for k in range(count):
            put_row(res, begin + k, residual_row(raw[begin + k - 1](), branch[k]))

    sweep([(stack, values[done - 2 :], kept_params(n_ref), w_ref)], 0, out_rows - done, emit)
    out = down_rows(flags, res, wd_ref, bd_ref, 0, height // 2)
    rows = height // 2
    for i in range(rows):
        row = jnp.where(flags[2] == 0, rows - 1 - i, i)
        send_ref[row] = jnp.where(even, other_ref[i], out[i])
        keep_ref[row] = jnp.where(even, out[i], other_ref[i])


def call(body, out_shape, scratch, flags, *groups, flops=0):
    vmem = pl.BlockSpec(memory_space=pltpu.VMEM)
    several = isinstance(out_shape, (list, tuple))
    args = [a for g in groups for a in (g if isinstance(g, tuple) else (g,))]
    moved = sum(a.size * a.dtype.itemsize for a in args)

    def kernel(flags_ref, *refs):
        rest = list(refs)
        given = [
            tuple(rest.pop(0) for _ in g) if isinstance(g, tuple) else rest.pop(0) for g in groups
        ]
        body(flags_ref, *given, *rest)

    return pl.pallas_call(
        kernel,
        out_shape=out_shape,
        in_specs=[pl.BlockSpec(memory_space=pltpu.SMEM)] + [vmem] * len(args),
        out_specs=[vmem] * len(out_shape) if several else vmem,
        scratch_shapes=scratch,
        cost_estimate=pl.CostEstimate(flops=flops, bytes_accessed=moved, transcendentals=0),
        compiler_params=pltpu.CompilerParams(vmem_limit_bytes=VMEM_LIMIT),
    )(flags, *args)


def turned(value, band):
    return jnp.where(band == 0, value[::-1], value)


def local(
    frames_in,
    gain_one,
    norm_bias_one,
    kernel_one,
    bias_one,
    gain_two,
    norm_bias_two,
    kernel_two,
    bias_two,
    kernel_down,
    bias_down,
):
    x = frames_in[:, 0]
    clips, height, width, channels = x.shape
    count = lax.axis_size("tm")
    bands = lax.axis_size("rows")
    assert clips == 2 and bands == 2 and count % 2 == 0 and height % 8 == 0
    cells = height * bands * width
    near = 3 * height // 8
    tail = height // TAIL
    position = lax.axis_index("tm")
    band = lax.axis_index("rows")
    side = position % 2
    flags = jnp.stack([side, (position < 2).astype(jnp.int32), band]).astype(jnp.int32)
    swap = [(i, i ^ 1) for i in range(count)]
    across = [(0, 1), (1, 0)]

    def onward(name, turn):
        wrap = name not in OPEN
        pairs = [(i, (i ^ turn) + 2) for i in range(count)]
        return [(i, j % count) for i, j in pairs if wrap or j < count]

    def swapped(v):
        return lax.ppermute(v, "tm", swap)

    def later(v, name):
        return lax.ppermute(v, "tm", onward(name, 0))

    def crossed(v, name):
        return lax.ppermute(v, "tm", onward(name, 1))

    def beside(v):
        return lax.ppermute(v, "rows", across)

    def row(v):
        return v.reshape(1, -1)

    def stack(rows):
        return [pltpu.VMEM((rows, width, 3 * channels), BF16)]

    def laid(n):
        return [pltpu.VMEM((9 * channels, n * channels), BF16)]

    def flops(rows, slots):
        return 2 * rows * width * 9 * channels * 2 * channels * slots

    def shape(*dims, dtype=BF16):
        return jax.ShapeDtypeStruct(dims, dtype)

    def kernel(body, *rest, **options):
        return call(functools.partial(body, cells), *rest, **options)

    split = near + 1
    sizes = (1, height - 1, 1, split - 1, height - split)
    parts = call(place_kernel, [shape(n, width, channels) for n in sizes], [], flags, x)
    own, other = tuple(parts[:2]), tuple(parts[2:])
    past = later(own[0], "own_on0"), later(own[1], "own_on1")
    mate = tuple(swapped(v) for v in other)
    partial = call(sums_kernel, shape(2, 8, channels, dtype=F32), [], flags, own, other)
    totals = partial + beside(partial)
    own_on_total = later(totals, "own_sums")
    cross_total = crossed(totals, "cross_sums")
    mate_total = swapped(totals)
    own = (beside(own[0]), *own)
    mate_on = tuple(later(v, f"mate_on{k}") for k, v in enumerate(mate))
    mate = (beside(mate[0]), *mate)
    past = (beside(past[0]), *past)

    norm_one = (row(gain_one), row(norm_bias_one))
    sums = shape(2, 8, channels, dtype=F32)
    params = shape(8, channels, dtype=F32)
    acc_shape = shape(height, width, 2 * channels, dtype=F32)
    acc = kernel(
        own_kernel,
        acc_shape,
        stack(height + 2) + laid(2),
        flags,
        own,
        totals,
        *norm_one,
        kernel_one,
        flops=flops(height, 1),
    )
    acc, cross_params, fall_edges = kernel(
        mates_kernel,
        [acc_shape, params, shape(2, width, channels)],
        stack(height + 2) + stack(height + 2) + laid(2) + laid(2),
        flags,
        own,
        mate,
        past,
        totals,
        mate_total,
        own_on_total,
        cross_total,
        *norm_one,
        kernel_one,
        acc,
        flops=flops(height, 2),
    )
    cross_edge = beside(mate_on[0])
    bias = row(bias_one)
    part = shape(near, width, channels)
    rest = shape(height - near, width, channels)
    early = shape(height - tail, width, channels)
    a_near, b1, edges, sums_near = kernel(
        near_kernel,
        [part, part, shape(2, 2, width, channels), sums],
        stack(near + 2) + laid(2),
        flags,
        (fall_edges, *own[1:]),
        mate[1:3],
        (cross_edge, *mate_on[:2]),
        cross_params,
        kernel_one,
        acc,
        bias,
        flops=flops(near, 1),
    )
    b1_on = later(b1, "b_on1")
    a1, b2, a2, partial = kernel(
        far_kernel,
        [early, rest, shape(tail, width, channels), sums],
        stack(height - near + 2) + [pltpu.VMEM(rest.shape, BF16)] + laid(2),
        flags,
        own[1:],
        mate[1:],
        mate_on,
        cross_params,
        kernel_one,
        acc,
        bias,
        a_near,
        sums_near,
        flops=flops(height - near, 1),
    )
    b2_on = later(b2, "b_on2")
    totals = partial + beside(partial)
    totals_on = later(totals, "hsums_on")
    a1_on = later(a1, "a_on1")
    a2_on = later(a2, "a_on2")
    edges = beside(edges)

    norm_two = (row(gain_two), row(norm_bias_two))
    acc = kernel(
        local_kernel,
        shape(height + 1, width, 2 * channels, dtype=F32),
        stack(height + 3) + stack(height + 3) + laid(2) + laid(2),
        flags,
        a1,
        a2,
        b1,
        b2,
        edges,
        totals,
        *norm_two,
        kernel_two,
        flops=flops(height + 1, 2),
    )
    down = turned(kernel_down, band).reshape(-1, channels)
    residual = [pltpu.VMEM((height + 2, width + 8, channels), F32)]
    b_edge = beside(b1_on[None, :2])
    out_shape = shape(height // 2, width // 2, channels)
    acc, out_b, a_params, w_a_on = kernel(
        second_kernel,
        [shape(height + 1, width, channels, dtype=F32), out_shape, params, shape(9 * channels, channels)],
        stack(height + 3) + residual + laid(2),
        flags,
        b1_on,
        b2_on,
        b_edge,
        totals_on,
        a1,
        a2,
        edges,
        totals,
        *norm_two,
        kernel_two,
        acc,
        row(bias_two),
        own,
        mate,
        down,
        row(bias_down),
        flops=flops(height + 1, 1),
    )
    a_edge = beside(a1_on[None, :2])
    ready = height - tail
    first_near = kernel(
        first_near_kernel,
        shape(ready, width, channels),
        stack(ready + 2),
        flags,
        a1_on,
        a_edge,
        a_params,
        a1,
        edges,
        w_a_on,
        acc,
        own,
        mate[:3],
        flops=flops(ready, 1),
    )
    sent, kept = kernel(
        first_far_kernel,
        [out_shape, out_shape],
        stack(tail + 3) + residual,
        flags,
        a1_on,
        a2_on,
        a_params,
        a1,
        a2,
        w_a_on,
        acc,
        first_near,
        out_b,
        own[1:],
        mate[1:],
        down,
        row(bias_down),
        flops=flops(tail + 1, 1),
    )
    received = swapped(sent)
    even = side == 0
    result = jnp.where(even, jnp.stack([kept, received]), jnp.stack([received, kept]))
    return result[:, None]


OPEN = ('b_on2','a_on1','a_on2')
TAIL = 2


def solution(mesh):
    placed = (P("groups", "tm", "rows", None, None),) + (P(),) * 10
    return jax.shard_map(
        local,
        mesh=mesh,
        in_specs=placed,
        out_specs=P("groups", "tm", "rows", None, None),
        check_vma=False,
    )
```

```python
import functools

import jax
import jax.numpy as jnp
from jax import lax
from jax.experimental import pallas as pl
from jax.experimental.pallas import tpu as pltpu
from jax.sharding import PartitionSpec as P


G = 32
EPSILON = 1e-06
F32 = jnp.float32
VMEM_LIMIT = 16 << 20
BF16 = jnp.bfloat16


def norm_params(totals, gain, bias, cells):
    channels = totals.shape[1]
    size = channels // G
    left = lax.broadcasted_iota(jnp.int32, (channels, channels), 0) // size
    right = lax.broadcasted_iota(jnp.int32, (channels, channels), 1) // size
    same = (left == right).astype(F32)
    grouped = jnp.dot(totals, same, precision=lax.Precision.HIGHEST, preferred_element_type=F32)
    grouped = grouped / (cells * size)
    mean = grouped[0:1]
    inverse = lax.rsqrt(grouped[1:2] - mean * mean + EPSILON)
    return mean, inverse * gain, bias


def keep_params(ref, params):
    for k, value in enumerate(params):
        ref[k : k + 1] = value


def kept_params(ref):
    return ref[0:1], ref[1:2], ref[2:3]


def fill_row(stack, r, values, params):
    mean, scale, bias = params
    width, channels = values.shape
    half = 0.5 * ((values.astype(F32) - mean) * scale + bias)
    normed = half + half * jnp.tanh(half)
    column = lax.broadcasted_iota(jnp.int32, (width, channels), 0)
    before = jnp.where(column == 0, 0.0, pltpu.roll(normed, 1, 0))
    after = jnp.where(column == width - 1, 0.0, pltpu.roll(normed, width - 1, 0))
    stack[r, :, 0:channels] = before.astype(BF16)
    stack[r, :, channels : 2 * channels] = normed.astype(BF16)
    stack[r, :, 2 * channels :] = after.astype(BF16)


def taps(stack, weights, start, count):
    rows = [
        jnp.concatenate([stack[r], stack[r + 1], stack[r + 2]], axis=1)
        for r in range(start, start + count)
    ]
    return jnp.dot(jnp.concatenate(rows, axis=0), weights, preferred_element_type=F32)


def steps(first, last):
    total = last - first
    size = 3 if total % 3 == 0 else 2
    return [(r, min(size, last - r)) for r in range(first, last, size)]


def sweep(frames, first, last, emit):
    filled = 0

    def fill(until):
        nonlocal filled
        for r in range(filled, until):
            for stack, values, params, _ in frames:
                if r < len(values):
                    fill_row(stack, r, values[r](), params)
                else:
                    stack[r] = jnp.zeros(stack.shape[1:], BF16)
        filled = max(filled, until)

    groups = steps(first, last)
    fill(sum(groups[0]) + 2)
    for k, (start, count) in enumerate(groups):
        part = sum(taps(stack, weights[...], start, count) for stack, _, _, weights in frames)
        if k + 1 < len(groups):
            fill(sum(groups[k + 1]) + 2)
        emit(start, count, part)


def reader(ref, r):
    return lambda: ref[r]


def rows_of(*refs):
    return [reader(ref, r) for ref in refs for r in range(ref.shape[0])]


def choose(flags, part, own, mate):
    def read():
        return jnp.where(flags[1] == 1, jnp.where(flags[0] == 0, own(), mate()), part())

    return read


def chosen(flags, parts, owns, mates):
    return [choose(flags, p, o, m) for p, o, m in zip(parts, owns, mates)]


def place_kernel(flags, x_ref, *parts):
    height = x_ref.shape[1]
    side, band = flags[0], flags[2]
    clips = [side] * height + [1 - side] * height
    rows = list(range(height)) * 2
    for part in parts:
        for k in range(part.shape[0]):
            r = rows.pop(0)
            part[k] = x_ref[clips.pop(0), jnp.where(band == 0, height - 1 - r, r)]


def lay_weights(out, k_ref, slot, band):
    channels = k_ref.shape[-1]
    for f in range(out.shape[1] // channels):
        frame = slot - f
        known = jnp.logical_and(frame >= 0, frame <= 2)
        frame = jnp.clip(frame, 0, 2)
        for a in range(3):
            tap = jnp.where(band == 0, 2 - a, a)
            for b in range(3):
                k = (3 * a + b) * channels
                block = jnp.where(known, k_ref[tap, b, frame], jnp.zeros((), BF16))
                out[k : k + channels, f * channels : (f + 1) * channels] = block


def sums_kernel(flags, own, other, out_ref):
    width, channels = own[0].shape[1:]
    for c, rows in enumerate((rows_of(*own), rows_of(*other))):
        total = jnp.zeros((8, channels), F32)
        square = jnp.zeros((8, channels), F32)
        for read in rows:
            v = read().astype(F32).reshape(width // 8, 8, channels)
            total += jnp.sum(v, axis=0)
            square += jnp.sum(v * v, axis=0)
        out_ref[c, 0:1] = jnp.sum(total, axis=0, keepdims=True)
        out_ref[c, 1:2] = jnp.sum(square, axis=0, keepdims=True)
        out_ref[c, 2:8] = jnp.zeros((6, channels), F32)


def own_kernel(cells, flags, own, t_ref, g_ref, c_ref, k_ref, acc_ref, stack, w_ref):
    height, width, _ = acc_ref.shape
    lay_weights(w_ref, k_ref, 2 + flags[0], flags[2])
    params = norm_params(t_ref[0], g_ref[...], c_ref[...], cells)

    def emit(start, count, part):
        acc_ref[start : start + count] = part.reshape(count, width, -1)

    sweep([(stack, rows_of(*own), params, w_ref)], 0, height, emit)


def mates_kernel(cells, flags, own, mate, past, to_ref, tm_ref, tp_ref, tq_ref, g_ref, c_ref, k_ref, in_ref, acc_ref, last_ref, edge_ref, xm, xp, wm, wp):
    height, width, _ = acc_ref.shape
    side = flags[0]
    first, even = flags[1] == 1, side == 0
    lay_weights(wm, k_ref, 3 - side, flags[2])
    lay_weights(wp, k_ref, side, flags[2])
    params = norm_params(tm_ref[1], g_ref[...], c_ref[...], cells)
    frames = [(xm, rows_of(*mate), params, wm)]
    start_totals = jnp.where(even, to_ref[0], tm_ref[1])
    totals = jnp.where(first, start_totals, tp_ref[0])
    params = norm_params(totals, g_ref[...], c_ref[...], cells)
    values = chosen(flags, rows_of(*past), rows_of(*own), rows_of(*mate))
    frames.append((xp, values, params, wp))

    def emit(start, count, part):
        acc_ref[start : start + count] = in_ref[start : start + count] + part.reshape(count, width, -1)

    sweep(frames, 0, height, emit)
    totals = jnp.where(first, start_totals, tq_ref[1])
    keep_params(last_ref, norm_params(totals, g_ref[...], c_ref[...], cells))
    edge_ref[0] = own[0][0]
    edge_ref[1] = mate[0][0]


def hidden_rows(stack, values, params, w_ref, in_ref, bias_ref, first, a_ref, b_ref, sum_ref):
    rows, width, channels = a_ref.shape
    both = 2 * channels
    bias = jnp.concatenate([bias_ref[...], bias_ref[...]], axis=1)
    total = jnp.zeros((8, both), F32)
    square = jnp.zeros((8, both), F32)

    def emit(start, count, part):
        nonlocal total, square
        begin = first + start
        part = part.reshape(count, width, both)
        hidden = (in_ref[begin : begin + count] + part + bias).astype(BF16)
        a_ref[start : start + count] = hidden[:, :, :channels]
        b_ref[start : start + count] = hidden[:, :, channels:]
        wide = hidden.astype(F32).reshape(count * width // 8, 8, both)
        total += jnp.sum(wide, axis=0)
        square += jnp.sum(wide * wide, axis=0)

    sweep([(stack, values, params, w_ref)], 0, rows, emit)
    total = jnp.sum(total, axis=0, keepdims=True)
    square = jnp.sum(square, axis=0, keepdims=True)
    for k in range(2):
        sum_ref[k, 0:1] = total[:, k * channels : (k + 1) * channels]
        sum_ref[k, 1:2] = square[:, k * channels : (k + 1) * channels]
        sum_ref[k, 2:8] = jnp.zeros((6, channels), F32)


def near_kernel(cells, flags, own, mate, past, n_ref, k_ref, in_ref, bias_ref, a_ref, b_ref, edge_ref, sum_ref, stack, w_ref):
    lay_weights(w_ref, k_ref, 1 - flags[0], flags[2])
    edges = own[0]
    owns = [reader(edges, 0)] + rows_of(*own[1:])
    mates = [reader(edges, 1)] + rows_of(*mate)
    values = chosen(flags, rows_of(*past), owns, mates)
    hidden_rows(stack, values, kept_params(n_ref), w_ref, in_ref, bias_ref, 0, a_ref, b_ref, sum_ref)
    edge_ref[0] = a_ref[0:2]
    edge_ref[1] = b_ref[0:2]


def far_kernel(cells, flags, own, mate, past, n_ref, k_ref, in_ref, bias_ref, near_ref, part_ref, a_ref, b_ref, c_ref, sum_ref, stack, held, w_ref):
    lay_weights(w_ref, k_ref, 1 - flags[0], flags[2])
    height = in_ref.shape[0]
    rows, early = b_ref.shape[0], near_ref.shape[0]
    values = chosen(flags, rows_of(*past), rows_of(*own), rows_of(*mate))
    first = height - rows
    hidden_rows(stack, values[first - 1 :], kept_params(n_ref), w_ref, in_ref, bias_ref, first, held, b_ref, sum_ref)
    sum_ref[...] += part_ref[...]
    whole = a_ref.shape[0]
    a_ref[0:early] = near_ref[...]
    a_ref[early:] = held[0 : whole - early]
    c_ref[...] = held[whole - early :]


def halves(edge, k, near, far):
    return [lambda: edge[k, 1], lambda: edge[k, 0]] + rows_of(near, far)


def local_kernel(cells, flags, a1, a2, b1, b2, e_ref, t_ref, g_ref, c_ref, k_ref, acc_ref, xa, xb, wa, wb):
    out_rows, width, _ = acc_ref.shape
    lay_weights(wa, k_ref, 2, flags[2])
    lay_weights(wb, k_ref, 3, flags[2])
    frames = []
    for k, (stack, near, far, weights) in enumerate(((xa, a1, a2, wa), (xb, b1, b2, wb))):
        params = norm_params(t_ref[k], g_ref[...], c_ref[...], cells)
        frames.append((stack, halves(e_ref, k, near, far), params, weights))

    def emit(start, count, part):
        acc_ref[start : start + count] = part.reshape(count, width, -1)

    sweep(frames, 0, out_rows, emit)


def either(flags, first, other):
    return lambda: jnp.where(flags[1] == 1, first(), other())


def residual_row(raw, branch):
    return (raw.astype(F32) + branch).astype(BF16)


def put_row(res, r, value):
    res[r, 0 : value.shape[0], :] = value.astype(F32)


def down_rows(flags, res, wd_ref, bd_ref, first, last):
    half = (res.shape[1] - 8) // 2
    band = flags[2]
    rows = []
    for i in range(first, last):
        cols = [
            res[2 * i + a + band, pl.ds(b, half, stride=2), :].astype(BF16)
            for a in range(3)
            for b in range(3)
        ]
        rows.append(jnp.concatenate(cols, axis=1))
    out = jnp.dot(jnp.concatenate(rows, axis=0), wd_ref[...], preferred_element_type=F32)
    out = (out + bd_ref[...]).astype(BF16)
    return out.reshape(last - first, half, -1)


def raw_rows(even, first, second):
    return [lambda f=f, s=s: jnp.where(even, f(), s()) for f, s in zip(first, second)]


def second_kernel(cells, flags, b1, b2, eb_ref, tp_ref, a1, a2, e_ref, t_ref, g_ref, c_ref, k_ref, in_ref, bias_ref, own, mate, wd_ref, bd_ref, acc_ref, out_ref, last_ref, wl_ref, stack, res, w_ref):
    out_rows, width, channels = acc_ref.shape
    height = out_rows - 1
    lay_weights(w_ref, k_ref, 1, flags[2])
    lay_weights(wl_ref, k_ref, 0, flags[2])
    params = norm_params(jnp.where(flags[1] == 1, t_ref[0], tp_ref[1]), g_ref[...], c_ref[...], cells)
    values = [
        either(flags, f, o) for f, o in zip(halves(e_ref, 0, a1, a2), halves(eb_ref, 0, b1, b2))
    ]
    raw = raw_rows(flags[0] == 0, rows_of(*mate), rows_of(*own))
    bias = jnp.concatenate([bias_ref[...], bias_ref[...]], axis=1)
    res[:, width:, :] = jnp.zeros((res.shape[0], res.shape[1] - width, channels), F32)
    res[out_rows] = jnp.zeros(res.shape[1:], F32)

    def emit(start, count, part):
        part = part.reshape(count, width, 2 * channels)
        branch = in_ref[start : start + count] + part + bias
        acc_ref[start : start + count] = branch[:, :, :channels]
        for k in range(count):
            put_row(res, start + k, residual_row(raw[start + k](), branch[k, :, channels:]))

    sweep([(stack, values, params, w_ref)], 0, out_rows, emit)
    out_ref[...] = down_rows(flags, res, wd_ref, bd_ref, 0, height // 2)
    params = norm_params(jnp.where(flags[1] == 1, t_ref[0], tp_ref[0]), g_ref[...], c_ref[...], cells)
    keep_params(last_ref, params)


def first_near_kernel(cells, flags, p1, ep_ref, n_ref, a1, e_ref, w_ref, in_ref, own, mate, out_ref, stack):
    rows, width, channels = out_ref.shape
    firsts = [lambda: e_ref[0, 1], lambda: e_ref[0, 0]] + rows_of(a1)
    others = [lambda: ep_ref[0, 1], lambda: ep_ref[0, 0]] + rows_of(p1)
    values = [either(flags, f, o) for f, o in zip(firsts, others)]
    raw = raw_rows(flags[0] == 0, rows_of(*own), rows_of(*mate))

    def emit(start, count, part):
        branch = in_ref[start : start + count] + part.reshape(count, width, channels)
        for k in range(count):
            out_ref[start + k] = residual_row(raw[start + k](), branch[k])

    sweep([(stack, values, kept_params(n_ref), w_ref)], 0, rows, emit)


def first_far_kernel(cells, flags, p1, p2, n_ref, a1, a2, w_ref, in_ref, near_ref, other_ref, own, mate, wd_ref, bd_ref, send_ref, keep_ref, stack, res):
    out_rows, width, channels = in_ref.shape
    height = out_rows - 1
    done = near_ref.shape[0]
    even = flags[0] == 0
    values = [either(flags, f, o) for f, o in zip(rows_of(a1, a2), rows_of(p1, p2))]
    raw = raw_rows(even, rows_of(*own), rows_of(*mate))
    res[:, width:, :] = jnp.zeros((res.shape[0], res.shape[1] - width, channels), F32)
    res[out_rows] = jnp.zeros(res.shape[1:], F32)
    for r in range(done):
        put_row(res, r, near_ref[r])

    def emit(start, count, part):
        begin = done + start
        branch = in_ref[begin : begin + count] + part.reshape(count, width, channels)
        for k in range(count):
            put_row(res, begin + k, residual_row(raw[begin + k - 1](), branch[k]))

    sweep([(stack, values[done - 2 :], kept_params(n_ref), w_ref)], 0, out_rows - done, emit)
    out = down_rows(flags, res, wd_ref, bd_ref, 0, height // 2)
    rows = height // 2
    for i in range(rows):
        row = jnp.where(flags[2] == 0, rows - 1 - i, i)
        send_ref[row] = jnp.where(even, other_ref[i], out[i])
        keep_ref[row] = jnp.where(even, out[i], other_ref[i])


def call(body, out_shape, scratch, flags, *groups, flops=0):
    vmem = pl.BlockSpec(memory_space=pltpu.VMEM)
    several = isinstance(out_shape, (list, tuple))
    args = [a for g in groups for a in (g if isinstance(g, tuple) else (g,))]
    moved = sum(a.size * a.dtype.itemsize for a in args)

    def kernel(flags_ref, *refs):
        rest = list(refs)
        given = [
            tuple(rest.pop(0) for _ in g) if isinstance(g, tuple) else rest.pop(0) for g in groups
        ]
        body(flags_ref, *given, *rest)

    return pl.pallas_call(
        kernel,
        out_shape=out_shape,
        in_specs=[pl.BlockSpec(memory_space=pltpu.SMEM)] + [vmem] * len(args),
        out_specs=[vmem] * len(out_shape) if several else vmem,
        scratch_shapes=scratch,
        cost_estimate=pl.CostEstimate(flops=flops, bytes_accessed=moved, transcendentals=0),
        compiler_params=pltpu.CompilerParams(vmem_limit_bytes=VMEM_LIMIT),
    )(flags, *args)


def turned(value, band):
    return jnp.where(band == 0, value[::-1], value)


def local(
    frames_in,
    gain_one,
    norm_bias_one,
    kernel_one,
    bias_one,
    gain_two,
    norm_bias_two,
    kernel_two,
    bias_two,
    kernel_down,
    bias_down,
):
    x = frames_in[:, 0]
    clips, height, width, channels = x.shape
    count = lax.axis_size("tm")
    bands = lax.axis_size("rows")
    assert clips == 2 and bands == 2 and count % 2 == 0 and height % 8 == 0
    cells = height * bands * width
    near = 3 * height // 8
    tail = height // TAIL
    position = lax.axis_index("tm")
    band = lax.axis_index("rows")
    side = position % 2
    flags = jnp.stack([side, (position < 2).astype(jnp.int32), band]).astype(jnp.int32)
    swap = [(i, i ^ 1) for i in range(count)]
    across = [(0, 1), (1, 0)]

    def onward(name, turn):
        wrap = name not in OPEN
        pairs = [(i, (i ^ turn) + 2) for i in range(count)]
        return [(i, j % count) for i, j in pairs if wrap or j < count]

    def swapped(v):
        return lax.ppermute(v, "tm", swap)

    def later(v, name):
        return lax.ppermute(v, "tm", onward(name, 0))

    def crossed(v, name):
        return lax.ppermute(v, "tm", onward(name, 1))

    def beside(v):
        return lax.ppermute(v, "rows", across)

    def row(v):
        return v.reshape(1, -1)

    def stack(rows):
        return [pltpu.VMEM((rows, width, 3 * channels), BF16)]

    def laid(n):
        return [pltpu.VMEM((9 * channels, n * channels), BF16)]

    def flops(rows, slots):
        return 2 * rows * width * 9 * channels * 2 * channels * slots

    def shape(*dims, dtype=BF16):
        return jax.ShapeDtypeStruct(dims, dtype)

    def kernel(body, *rest, **options):
        return call(functools.partial(body, cells), *rest, **options)

    split = near + 1
    sizes = (1, height - 1, split, height - split)
    parts = call(place_kernel, [shape(n, width, channels) for n in sizes], [], flags, x)
    own, other = tuple(parts[:2]), tuple(parts[2:])
    past = later(own[0], "own_on0"), later(own[1], "own_on1")
    mate = tuple(swapped(v) for v in other)
    partial = call(sums_kernel, shape(2, 8, channels, dtype=F32), [], flags, own, other)
    totals = partial + beside(partial)
    own_on_total = later(totals, "own_sums")
    cross_total = crossed(totals, "cross_sums")
    mate_total = swapped(totals)
    mate_on = tuple(
        later(v, f"mate_on{k}") for k, v in enumerate((mate[0][:1], mate[0][1:], mate[1]))
    )
    own = (beside(own[0]), *own)
    mate = (beside(mate[0][:1]), *mate)
    past = (beside(past[0]), *past)

    norm_one = (row(gain_one), row(norm_bias_one))
    sums = shape(2, 8, channels, dtype=F32)
    params = shape(8, channels, dtype=F32)
    acc_shape = shape(height, width, 2 * channels, dtype=F32)
    acc = kernel(
        own_kernel,
        acc_shape,
        stack(height + 2) + laid(2),
        flags,
        own,
        totals,
        *norm_one,
        kernel_one,
        flops=flops(height, 1),
    )
    acc, cross_params, fall_edges = kernel(
        mates_kernel,
        [acc_shape, params, shape(2, width, channels)],
        stack(height + 2) + stack(height + 2) + laid(2) + laid(2),
        flags,
        own,
        mate,
        past,
        totals,
        mate_total,
        own_on_total,
        cross_total,
        *norm_one,
        kernel_one,
        acc,
        flops=flops(height, 2),
    )
    cross_edge = beside(mate_on[0])
    bias = row(bias_one)
    part = shape(near, width, channels)
    rest = shape(height - near, width, channels)
    early = shape(height - tail, width, channels)
    a_near, b1, edges, sums_near = kernel(
        near_kernel,
        [part, part, shape(2, 2, width, channels), sums],
        stack(near + 2) + laid(2),
        flags,
        (fall_edges, *own[1:]),
        mate[1:2],
        (cross_edge, *mate_on[:2]),
        cross_params,
        kernel_one,
        acc,
        bias,
        flops=flops(near, 1),
    )
    b1_on = later(b1, "b_on1")
    a1, b2, a2, partial = kernel(
        far_kernel,
        [early, rest, shape(tail, width, channels), sums],
        stack(height - near + 2) + [pltpu.VMEM(rest.shape, BF16)] + laid(2),
        flags,
        own[1:],
        mate[1:],
        mate_on,
        cross_params,
        kernel_one,
        acc,
        bias,
        a_near,
        sums_near,
        flops=flops(height - near, 1),
    )
    b2_on = later(b2, "b_on2")
    totals = partial + beside(partial)
    totals_on = later(totals, "hsums_on")
    a1_on = later(a1, "a_on1")
    a2_on = later(a2, "a_on2")
    edges = beside(edges)

    norm_two = (row(gain_two), row(norm_bias_two))
    acc = kernel(
        local_kernel,
        shape(height + 1, width, 2 * channels, dtype=F32),
        stack(height + 3) + stack(height + 3) + laid(2) + laid(2),
        flags,
        a1,
        a2,
        b1,
        b2,
        edges,
        totals,
        *norm_two,
        kernel_two,
        flops=flops(height + 1, 2),
    )
    down = turned(kernel_down, band).reshape(-1, channels)
    residual = [pltpu.VMEM((height + 2, width + 8, channels), F32)]
    b_edge = beside(b1_on[None, :2])
    out_shape = shape(height // 2, width // 2, channels)
    acc, out_b, a_params, w_a_on = kernel(
        second_kernel,
        [shape(height + 1, width, channels, dtype=F32), out_shape, params, shape(9 * channels, channels)],
        stack(height + 3) + residual + laid(2),
        flags,
        b1_on,
        b2_on,
        b_edge,
        totals_on,
        a1,
        a2,
        edges,
        totals,
        *norm_two,
        kernel_two,
        acc,
        row(bias_two),
        own,
        mate,
        down,
        row(bias_down),
        flops=flops(height + 1, 1),
    )
    a_edge = beside(a1_on[None, :2])
    ready = height - tail
    first_near = kernel(
        first_near_kernel,
        shape(ready, width, channels),
        stack(ready + 2),
        flags,
        a1_on,
        a_edge,
        a_params,
        a1,
        edges,
        w_a_on,
        acc,
        own,
        mate[:2],
        flops=flops(ready, 1),
    )
    sent, kept = kernel(
        first_far_kernel,
        [out_shape, out_shape],
        stack(tail + 3) + residual,
        flags,
        a1_on,
        a2_on,
        a_params,
        a1,
        a2,
        w_a_on,
        acc,
        first_near,
        out_b,
        own[1:],
        mate[1:],
        down,
        row(bias_down),
        flops=flops(tail + 1, 1),
    )
    received = swapped(sent)
    even = side == 0
    result = jnp.where(even, jnp.stack([kept, received]), jnp.stack([received, kept]))
    return result[:, None]


OPEN = ('b_on2','a_on1','a_on2')
TAIL = 2


def solution(mesh):
    placed = (P("groups", "tm", "rows", None, None),) + (P(),) * 10
    return jax.shard_map(
        local,
        mesh=mesh,
        in_specs=placed,
        out_specs=P("groups", "tm", "rows", None, None),
        check_vma=False,
    )
```

```python
import functools

import jax
import jax.numpy as jnp
from jax import lax
from jax.experimental import pallas as pl
from jax.experimental.pallas import tpu as pltpu
from jax.sharding import PartitionSpec as P


G = 32
EPSILON = 1e-06
F32 = jnp.float32
VMEM_LIMIT = 16 << 20
BF16 = jnp.bfloat16


def norm_params(totals, gain, bias, cells):
    channels = totals.shape[1]
    size = channels // G
    left = lax.broadcasted_iota(jnp.int32, (channels, channels), 0) // size
    right = lax.broadcasted_iota(jnp.int32, (channels, channels), 1) // size
    same = (left == right).astype(F32)
    grouped = jnp.dot(totals, same, precision=lax.Precision.HIGHEST, preferred_element_type=F32)
    grouped = grouped / (cells * size)
    mean = grouped[0:1]
    inverse = lax.rsqrt(jnp.maximum(grouped[1:2] - mean * mean, 0.0) + EPSILON)
    return mean, inverse * gain, bias


def keep_params(ref, params):
    for k, value in enumerate(params):
        ref[k : k + 1] = value


def kept_params(ref):
    return ref[0:1], ref[1:2], ref[2:3]


def fill_row(stack, r, values, params):
    mean, scale, bias = params
    width, channels = values.shape
    half = 0.5 * ((values.astype(F32) - mean) * scale + bias)
    normed = half + half * jnp.tanh(half)
    column = lax.broadcasted_iota(jnp.int32, (width, channels), 0)
    before = jnp.where(column == 0, 0.0, pltpu.roll(normed, 1, 0))
    after = jnp.where(column == width - 1, 0.0, pltpu.roll(normed, width - 1, 0))
    stack[r, :, 0:channels] = before.astype(BF16)
    stack[r, :, channels : 2 * channels] = normed.astype(BF16)
    stack[r, :, 2 * channels :] = after.astype(BF16)


def taps(stack, weights, start, count):
    rows = [
        jnp.concatenate([stack[r], stack[r + 1], stack[r + 2]], axis=1)
        for r in range(start, start + count)
    ]
    return jnp.dot(jnp.concatenate(rows, axis=0), weights, preferred_element_type=F32)


def steps(first, last):
    total = last - first
    size = -(-total // 2) if total > 5 else total
    return [(r, min(size, last - r)) for r in range(first, last, size)]


def sweep(frames, first, last, emit):
    filled = 0

    def fill(until):
        nonlocal filled
        for r in range(filled, until):
            for stack, values, params, _ in frames:
                if r < len(values):
                    fill_row(stack, r, values[r](), params)
                else:
                    stack[r] = jnp.zeros(stack.shape[1:], BF16)
        filled = max(filled, until)

    groups = steps(first, last)
    fill(sum(groups[0]) + 2)
    for k, (start, count) in enumerate(groups):
        part = sum(taps(stack, weights[...], start, count) for stack, _, _, weights in frames)
        if k + 1 < len(groups):
            fill(sum(groups[k + 1]) + 2)
        emit(start, count, part)


def reader(ref, r):
    return lambda: ref[r]


def rows_of(*refs):
    return [reader(ref, r) for ref in refs for r in range(ref.shape[0])]


def choose(flags, part, own, mate):
    def read():
        return jnp.where(flags[1] == 1, jnp.where(flags[0] == 0, own(), mate()), part())

    return read


def chosen(flags, parts, owns, mates):
    return [choose(flags, p, o, m) for p, o, m in zip(parts, owns, mates)]


def place_kernel(flags, x_ref, *parts):
    height = x_ref.shape[1]
    side, band = flags[0], flags[2]
    clips = [side] * height + [1 - side] * height
    rows = list(range(height)) * 2
    for part in parts:
        for k in range(part.shape[0]):
            r = rows.pop(0)
            part[k] = x_ref[clips.pop(0), jnp.where(band == 0, height - 1 - r, r)]


def lay_weights(out, k_ref, slot, band):
    channels = k_ref.shape[-1]
    for f in range(out.shape[1] // channels):
        frame = slot - f
        known = jnp.logical_and(frame >= 0, frame <= 2)
        frame = jnp.clip(frame, 0, 2)
        for a in range(3):
            tap = jnp.where(band == 0, 2 - a, a)
            for b in range(3):
                k = (3 * a + b) * channels
                block = jnp.where(known, k_ref[tap, b, frame], jnp.zeros((), BF16))
                out[k : k + channels, f * channels : (f + 1) * channels] = block


def sums_kernel(flags, own, other, out_ref):
    width, channels = own[0].shape[1:]
    for c, rows in enumerate((rows_of(*own), rows_of(*other))):
        total = jnp.zeros((8, channels), F32)
        square = jnp.zeros((8, channels), F32)
        for read in rows:
            v = read().astype(F32).reshape(width // 8, 8, channels)
            total += jnp.sum(v, axis=0)
            square += jnp.sum(v * v, axis=0)
        out_ref[c, 0:1] = jnp.sum(total, axis=0, keepdims=True)
        out_ref[c, 1:2] = jnp.sum(square, axis=0, keepdims=True)
        out_ref[c, 2:8] = jnp.zeros((6, channels), F32)


def own_kernel(cells, flags, own, t_ref, g_ref, c_ref, k_ref, acc_ref, stack, w_ref):
    height, width, _ = acc_ref.shape
    lay_weights(w_ref, k_ref, 2 + flags[0], flags[2])
    params = norm_params(t_ref[0], g_ref[...], c_ref[...], cells)

    def emit(start, count, part):
        acc_ref[start : start + count] = part.reshape(count, width, -1)

    sweep([(stack, rows_of(*own), params, w_ref)], 0, height, emit)


def mates_kernel(cells, flags, own, mate, past, to_ref, tm_ref, tp_ref, tq_ref, g_ref, c_ref, k_ref, in_ref, acc_ref, last_ref, edge_ref, xm, xp, wm, wp):
    height, width, _ = acc_ref.shape
    side = flags[0]
    first, even = flags[1] == 1, side == 0
    lay_weights(wm, k_ref, 3 - side, flags[2])
    lay_weights(wp, k_ref, side, flags[2])
    params = norm_params(tm_ref[1], g_ref[...], c_ref[...], cells)
    frames = [(xm, rows_of(*mate), params, wm)]
    start_totals = jnp.where(even, to_ref[0], tm_ref[1])
    totals = jnp.where(first, start_totals, tp_ref[0])
    params = norm_params(totals, g_ref[...], c_ref[...], cells)
    values = chosen(flags, rows_of(*past), rows_of(*own), rows_of(*mate))
    frames.append((xp, values, params, wp))

    def emit(start, count, part):
        acc_ref[start : start + count] = in_ref[start : start + count] + part.reshape(count, width, -1)

    sweep(frames, 0, height, emit)
    totals = jnp.where(first, start_totals, tq_ref[1])
    keep_params(last_ref, norm_params(totals, g_ref[...], c_ref[...], cells))
    edge_ref[0] = own[0][0]
    edge_ref[1] = mate[0][0]


def hidden_rows(stack, values, params, w_ref, in_ref, bias_ref, first, a_ref, b_ref, sum_ref):
    rows, width, channels = a_ref.shape
    both = 2 * channels
    bias = jnp.concatenate([bias_ref[...], bias_ref[...]], axis=1)
    total = jnp.zeros((8, both), F32)
    square = jnp.zeros((8, both), F32)

    def emit(start, count, part):
        nonlocal total, square
        begin = first + start
        part = part.reshape(count, width, both)
        hidden = (in_ref[begin : begin + count] + part + bias).astype(BF16)
        a_ref[start : start + count] = hidden[:, :, :channels]
        b_ref[start : start + count] = hidden[:, :, channels:]
        wide = hidden.astype(F32).reshape(count * width // 8, 8, both)
        total += jnp.sum(wide, axis=0)
        square += jnp.sum(wide * wide, axis=0)

    sweep([(stack, values, params, w_ref)], 0, rows, emit)
    total = jnp.sum(total, axis=0, keepdims=True)
    square = jnp.sum(square, axis=0, keepdims=True)
    for k in range(2):
        sum_ref[k, 0:1] = total[:, k * channels : (k + 1) * channels]
        sum_ref[k, 1:2] = square[:, k * channels : (k + 1) * channels]
        sum_ref[k, 2:8] = jnp.zeros((6, channels), F32)


def near_kernel(cells, flags, own, mate, past, n_ref, k_ref, in_ref, bias_ref, a_ref, b_ref, edge_ref, sum_ref, stack, w_ref):
    lay_weights(w_ref, k_ref, 1 - flags[0], flags[2])
    edges = own[0]
    owns = [reader(edges, 0)] + rows_of(*own[1:])
    mates = [reader(edges, 1)] + rows_of(*mate)
    values = chosen(flags, rows_of(*past), owns, mates)
    hidden_rows(stack, values, kept_params(n_ref), w_ref, in_ref, bias_ref, 0, a_ref, b_ref, sum_ref)
    edge_ref[0] = a_ref[0:2]
    edge_ref[1] = b_ref[0:2]


def far_kernel(cells, flags, own, mate, past, n_ref, k_ref, in_ref, bias_ref, near_ref, part_ref, a_ref, b_ref, c_ref, sum_ref, stack, held, w_ref):
    lay_weights(w_ref, k_ref, 1 - flags[0], flags[2])
    height = in_ref.shape[0]
    rows, early = b_ref.shape[0], near_ref.shape[0]
    values = chosen(flags, rows_of(*past), rows_of(*own), rows_of(*mate))
    first = height - rows
    hidden_rows(stack, values[first - 1 :], kept_params(n_ref), w_ref, in_ref, bias_ref, first, held, b_ref, sum_ref)
    sum_ref[...] += part_ref[...]
    whole = a_ref.shape[0]
    a_ref[0:early] = near_ref[...]
    a_ref[early:] = held[0 : whole - early]
    c_ref[...] = held[whole - early :]


def halves(edge, k, near, far):
    return [lambda: edge[k, 1], lambda: edge[k, 0]] + rows_of(near, far)


def local_kernel(cells, flags, a1, a2, b1, b2, e_ref, t_ref, g_ref, c_ref, k_ref, acc_ref, xa, xb, wa, wb):
    out_rows, width, _ = acc_ref.shape
    lay_weights(wa, k_ref, 2, flags[2])
    lay_weights(wb, k_ref, 3, flags[2])
    frames = []
    for k, (stack, near, far, weights) in enumerate(((xa, a1, a2, wa), (xb, b1, b2, wb))):
        params = norm_params(t_ref[k], g_ref[...], c_ref[...], cells)
        frames.append((stack, halves(e_ref, k, near, far), params, weights))

    def emit(start, count, part):
        acc_ref[start : start + count] = part.reshape(count, width, -1)

    sweep(frames, 0, out_rows, emit)


def either(flags, first, other):
    return lambda: jnp.where(flags[1] == 1, first(), other())


def residual_row(raw, branch):
    return (raw.astype(F32) + branch).astype(BF16)


def put_row(res, r, value):
    res[r, 0 : value.shape[0], :] = value.astype(F32)


def down_rows(flags, res, wd_ref, bd_ref, first, last):
    half = (res.shape[1] - 8) // 2
    band = flags[2]
    rows = []
    for i in range(first, last):
        cols = [
            res[2 * i + a + band, pl.ds(b, half, stride=2), :].astype(BF16)
            for a in range(3)
            for b in range(3)
        ]
        rows.append(jnp.concatenate(cols, axis=1))
    out = jnp.dot(jnp.concatenate(rows, axis=0), wd_ref[...], preferred_element_type=F32)
    out = (out + bd_ref[...]).astype(BF16)
    return out.reshape(last - first, half, -1)


def raw_rows(even, first, second):
    return [lambda f=f, s=s: jnp.where(even, f(), s()) for f, s in zip(first, second)]


def second_kernel(cells, flags, b1, b2, eb_ref, tp_ref, a1, a2, e_ref, t_ref, g_ref, c_ref, k_ref, in_ref, bias_ref, own, mate, wd_ref, bd_ref, acc_ref, out_ref, last_ref, wl_ref, stack, res, w_ref):
    out_rows, width, channels = acc_ref.shape
    height = out_rows - 1
    lay_weights(w_ref, k_ref, 1, flags[2])
    lay_weights(wl_ref, k_ref, 0, flags[2])
    params = norm_params(jnp.where(flags[1] == 1, t_ref[0], tp_ref[1]), g_ref[...], c_ref[...], cells)
    values = [
        either(flags, f, o) for f, o in zip(halves(e_ref, 0, a1, a2), halves(eb_ref, 0, b1, b2))
    ]
    raw = raw_rows(flags[0] == 0, rows_of(*mate), rows_of(*own))
    bias = jnp.concatenate([bias_ref[...], bias_ref[...]], axis=1)
    res[:, width:, :] = jnp.zeros((res.shape[0], res.shape[1] - width, channels), F32)
    res[out_rows] = jnp.zeros(res.shape[1:], F32)

    def emit(start, count, part):
        part = part.reshape(count, width, 2 * channels)
        branch = in_ref[start : start + count] + part + bias
        acc_ref[start : start + count] = branch[:, :, :channels]
        for k in range(count):
            put_row(res, start + k, residual_row(raw[start + k](), branch[k, :, channels:]))

    sweep([(stack, values, params, w_ref)], 0, out_rows, emit)
    out_ref[...] = down_rows(flags, res, wd_ref, bd_ref, 0, height // 2)
    params = norm_params(jnp.where(flags[1] == 1, t_ref[0], tp_ref[0]), g_ref[...], c_ref[...], cells)
    keep_params(last_ref, params)


def first_near_kernel(cells, flags, p1, ep_ref, n_ref, a1, e_ref, w_ref, in_ref, own, mate, out_ref, stack):
    rows, width, channels = out_ref.shape
    firsts = [lambda: e_ref[0, 1], lambda: e_ref[0, 0]] + rows_of(a1)
    others = [lambda: ep_ref[0, 1], lambda: ep_ref[0, 0]] + rows_of(p1)
    values = [either(flags, f, o) for f, o in zip(firsts, others)]
    raw = raw_rows(flags[0] == 0, rows_of(*own), rows_of(*mate))

    def emit(start, count, part):
        branch = in_ref[start : start + count] + part.reshape(count, width, channels)
        for k in range(count):
            out_ref[start + k] = residual_row(raw[start + k](), branch[k])

    sweep([(stack, values, kept_params(n_ref), w_ref)], 0, rows, emit)


def first_far_kernel(cells, flags, p1, p2, n_ref, a1, a2, w_ref, in_ref, near_ref, other_ref, own, mate, wd_ref, bd_ref, send_ref, keep_ref, stack, res):
    out_rows, width, channels = in_ref.shape
    height = out_rows - 1
    done = near_ref.shape[0]
    even = flags[0] == 0
    values = [either(flags, f, o) for f, o in zip(rows_of(a1, a2), rows_of(p1, p2))]
    raw = raw_rows(even, rows_of(*own), rows_of(*mate))
    res[:, width:, :] = jnp.zeros((res.shape[0], res.shape[1] - width, channels), F32)
    res[out_rows] = jnp.zeros(res.shape[1:], F32)
    for r in range(done):
        put_row(res, r, near_ref[r])

    def emit(start, count, part):
        begin = done + start
        branch = in_ref[begin : begin + count] + part.reshape(count, width, channels)
        for k in range(count):
            put_row(res, begin + k, residual_row(raw[begin + k - 1](), branch[k]))

    sweep([(stack, values[done - 2 :], kept_params(n_ref), w_ref)], 0, out_rows - done, emit)
    out = down_rows(flags, res, wd_ref, bd_ref, 0, height // 2)
    rows = height // 2
    for i in range(rows):
        row = jnp.where(flags[2] == 0, rows - 1 - i, i)
        send_ref[row] = jnp.where(even, other_ref[i], out[i])
        keep_ref[row] = jnp.where(even, out[i], other_ref[i])


def call(body, out_shape, scratch, flags, *groups, flops=0):
    vmem = pl.BlockSpec(memory_space=pltpu.VMEM)
    several = isinstance(out_shape, (list, tuple))
    args = [a for g in groups for a in (g if isinstance(g, tuple) else (g,))]
    moved = sum(a.size * a.dtype.itemsize for a in args)

    def kernel(flags_ref, *refs):
        rest = list(refs)
        given = [
            tuple(rest.pop(0) for _ in g) if isinstance(g, tuple) else rest.pop(0) for g in groups
        ]
        body(flags_ref, *given, *rest)

    return pl.pallas_call(
        kernel,
        out_shape=out_shape,
        in_specs=[pl.BlockSpec(memory_space=pltpu.SMEM)] + [vmem] * len(args),
        out_specs=[vmem] * len(out_shape) if several else vmem,
        scratch_shapes=scratch,
        cost_estimate=pl.CostEstimate(flops=flops, bytes_accessed=moved, transcendentals=0),
        compiler_params=pltpu.CompilerParams(vmem_limit_bytes=VMEM_LIMIT),
    )(flags, *args)


def turned(value, band):
    return jnp.where(band == 0, value[::-1], value)


def local(
    frames_in,
    gain_one,
    norm_bias_one,
    kernel_one,
    bias_one,
    gain_two,
    norm_bias_two,
    kernel_two,
    bias_two,
    kernel_down,
    bias_down,
):
    x = frames_in[:, 0]
    clips, height, width, channels = x.shape
    count = lax.axis_size("tm")
    bands = lax.axis_size("rows")
    assert clips == 2 and bands == 2 and count % 2 == 0 and height % 8 == 0
    cells = height * bands * width
    near = 3 * height // 8
    tail = 3 * height // 8
    position = lax.axis_index("tm")
    band = lax.axis_index("rows")
    side = position % 2
    flags = jnp.stack([side, (position < 2).astype(jnp.int32), band]).astype(jnp.int32)
    swap = [(i, i ^ 1) for i in range(count)]
    across = [(0, 1), (1, 0)]

    def onward(name, turn):
        wrap = name not in OPEN
        pairs = [(i, (i ^ turn) + 2) for i in range(count)]
        return [(i, j % count) for i, j in pairs if wrap or j < count]

    def swapped(v):
        return lax.ppermute(v, "tm", swap)

    def later(v, name):
        return lax.ppermute(v, "tm", onward(name, 0))

    def crossed(v, name):
        return lax.ppermute(v, "tm", onward(name, 1))

    def beside(v):
        return lax.ppermute(v, "rows", across)

    def row(v):
        return v.reshape(1, -1)

    def stack(rows):
        return [pltpu.VMEM((rows, width, 3 * channels), BF16)]

    def laid(n):
        return [pltpu.VMEM((9 * channels, n * channels), BF16)]

    def flops(rows, slots):
        return 2 * rows * width * 9 * channels * 2 * channels * slots

    def shape(*dims, dtype=BF16):
        return jax.ShapeDtypeStruct(dims, dtype)

    def kernel(body, *rest, **options):
        return call(functools.partial(body, cells), *rest, **options)

    split = near + 1
    sizes = (1, height - 1, split, height - split)
    parts = call(place_kernel, [shape(n, width, channels) for n in sizes], [], flags, x)
    own, other = tuple(parts[:2]), tuple(parts[2:])
    past = later(own[0], "own_on0"), later(own[1], "own_on1")
    mate = tuple(swapped(v) for v in other)
    partial = call(sums_kernel, shape(2, 8, channels, dtype=F32), [], flags, own, other)
    totals = partial + beside(partial)
    own_on_total = later(totals, "own_sums")
    cross_total = crossed(totals, "cross_sums")
    mate_total = swapped(totals)
    mate_on = tuple(
        later(v, f"mate_on{k}") for k, v in enumerate((mate[0][:1], mate[0][1:], mate[1]))
    )
    own = (beside(own[0]), *own)
    mate = (beside(mate[0][:1]), *mate)
    past = (beside(past[0]), *past)

    norm_one = (row(gain_one), row(norm_bias_one))
    sums = shape(2, 8, channels, dtype=F32)
    params = shape(8, channels, dtype=F32)
    acc_shape = shape(height, width, 2 * channels, dtype=F32)
    acc = kernel(
        own_kernel,
        acc_shape,
        stack(height + 2) + laid(2),
        flags,
        own,
        totals,
        *norm_one,
        kernel_one,
        flops=flops(height, 1),
    )
    acc, cross_params, fall_edges = kernel(
        mates_kernel,
        [acc_shape, params, shape(2, width, channels)],
        stack(height + 2) + stack(height + 2) + laid(2) + laid(2),
        flags,
        own,
        mate,
        past,
        totals,
        mate_total,
        own_on_total,
        cross_total,
        *norm_one,
        kernel_one,
        acc,
        flops=flops(height, 2),
    )
    cross_edge = beside(mate_on[0])
    bias = row(bias_one)
    part = shape(near, width, channels)
    rest = shape(height - near, width, channels)
    early = shape(height - tail, width, channels)
    a_near, b1, edges, sums_near = kernel(
        near_kernel,
        [part, part, shape(2, 2, width, channels), sums],
        stack(near + 2) + laid(2),
        flags,
        (fall_edges, *own[1:]),
        mate[1:2],
        (cross_edge, *mate_on[:2]),
        cross_params,
        kernel_one,
        acc,
        bias,
        flops=flops(near, 1),
    )
    b1_on = later(b1, "b_on1")
    a1, b2, a2, partial = kernel(
        far_kernel,
        [early, rest, shape(tail, width, channels), sums],
        stack(height - near + 2) + [pltpu.VMEM(rest.shape, BF16)] + laid(2),
        flags,
        own[1:],
        mate[1:],
        mate_on,
        cross_params,
        kernel_one,
        acc,
        bias,
        a_near,
        sums_near,
        flops=flops(height - near, 1),
    )
    b2_on = later(b2, "b_on2")
    totals = partial + beside(partial)
    totals_on = later(totals, "hsums_on")
    a1_on = later(a1, "a_on1")
    a2_on = later(a2, "a_on2")
    edges = beside(edges)

    norm_two = (row(gain_two), row(norm_bias_two))
    acc = kernel(
        local_kernel,
        shape(height + 1, width, 2 * channels, dtype=F32),
        stack(height + 3) + stack(height + 3) + laid(2) + laid(2),
        flags,
        a1,
        a2,
        b1,
        b2,
        edges,
        totals,
        *norm_two,
        kernel_two,
        flops=flops(height + 1, 2),
    )
    down = turned(kernel_down, band).reshape(-1, channels)
    residual = [pltpu.VMEM((height + 2, width + 8, channels), F32)]
    b_edge = beside(b1_on[None, :2])
    out_shape = shape(height // 2, width // 2, channels)
    acc, out_b, a_params, w_a_on = kernel(
        second_kernel,
        [shape(height + 1, width, channels, dtype=F32), out_shape, params, shape(9 * channels, channels)],
        stack(height + 3) + residual + laid(2),
        flags,
        b1_on,
        b2_on,
        b_edge,
        totals_on,
        a1,
        a2,
        edges,
        totals,
        *norm_two,
        kernel_two,
        acc,
        row(bias_two),
        own,
        mate,
        down,
        row(bias_down),
        flops=flops(height + 1, 1),
    )
    a_edge = beside(a1_on[None, :2])
    ready = height - tail
    first_near = kernel(
        first_near_kernel,
        shape(ready, width, channels),
        stack(ready + 2),
        flags,
        a1_on,
        a_edge,
        a_params,
        a1,
        edges,
        w_a_on,
        acc,
        own,
        mate[:2],
        flops=flops(ready, 1),
    )
    sent, kept = kernel(
        first_far_kernel,
        [out_shape, out_shape],
        stack(tail + 3) + residual,
        flags,
        a1_on,
        a2_on,
        a_params,
        a1,
        a2,
        w_a_on,
        acc,
        first_near,
        out_b,
        own[1:],
        mate[1:],
        down,
        row(bias_down),
        flops=flops(tail + 1, 1),
    )
    received = swapped(sent)
    even = side == 0
    result = jnp.where(even, jnp.stack([kept, received]), jnp.stack([received, kept]))
    return result[:, None]


OPEN = ('b_on2', 'a_on2')


def solution(mesh):
    placed = (P("groups", "tm", "rows", None, None),) + (P(),) * 10
    return jax.shard_map(
        local,
        mesh=mesh,
        in_specs=placed,
        out_specs=P("groups", "tm", "rows", None, None),
        check_vma=False,
    )
```
